32 devices in a mesh: segment: 2 (over x), expert: 16 (over z, y, core).
Axes of the slice: x: 2, y: 2, z: 4, core: 2. Of those that a mesh axis runs over, the one named last changes fastest.
Arguments:
- handoff: bfloat16 [2, 1024, 4096], P('segment', 'expert'), may hold values from -6 to 6
- saved_inputs: bfloat16 [2, 1024, 4096], P('segment', 'expert'), may hold values from -6 to 6
- cotangent: bfloat16 [2, 1024, 4096], P('segment', 'expert'), may hold values from -6 to 6
- ids_forward: int32 [2, 1024, 2], P('segment', 'expert'), may hold values from 0 to 63, all different within a row; in each aligned block of 64 rows (0 to 63, 64 to 127, ..., all dimensions but the last counted through in order) at most 5 rows name the same one
- gates_forward: float32 [2, 1024, 2], P('segment', 'expert'), may hold values from 0.25 to 1
- ids_backward: int32 [2, 1024, 2], P('segment', 'expert'), may hold values from 0 to 63, all different within a row; in each aligned block of 64 rows (0 to 63, 64 to 127, ..., all dimensions but the last counted through in order) at most 5 rows name the same one
- gates_backward: float32 [2, 1024, 2], P('segment', 'expert'), may hold values from 0.25 to 1
- weight_in: bfloat16 [2, 4096, 2048], P('segment', None, 'expert'), may hold values from -0.09375 to 0.09375
- weight_out: bfloat16 [2, 2048, 4096], P('segment', 'expert'), may hold values from -0.125 to 0.125
Outputs:
- expert_mix: bfloat16 [2, 1024, 4096], P('segment', 'expert')
- input_grads: bfloat16 [2, 1024, 4096], P('segment', 'expert')
The draws below stay inside these ranges and needn't reach their ends.
Inputs may be any that keep to these rules, and one draw needn't show every extreme that they name: `ids_forward`: the two experts of a row differ; within the rows of one device no expert is named by more than 5 rows. `ids_backward`: the two experts of a row differ; within the rows of one device no expert is named by more than 5 rows.
All inputs are finite; a program needn't handle non-finite values.
Results may differ from the reference program's by a relative error of at most 0.013.
Values may be sent and summed in bfloat16 or wider, within the bound.
A program may use at most 128 MiB of HBM per device.

```python
import math
from functools import partial
import jax
import jax.numpy as jnp
import numpy as np
from jax import lax

D = 4096
FF = 2048
ALL_EXPERTS = 64
GROUP = 16
ROWS_DEV = 64
CAP = 5
EXPERTS = 1
ROWS = 1024
SEGMENTS = 2
N_EXPERT = 16


def levels(own_key, extent, shards, low, high):
    def one(dim, shards_of):
        draws = jax.random.uniform(jax.random.fold_in(jax.random.fold_in(own_key, 6), dim), (shards_of,), jnp.float32, low / len(shards), high / len(shards))
        return jnp.repeat(jnp.exp(draws), extent[dim] // shards_of).reshape((-1,) + (1,) * (len(extent) - dim - 1))

    factor_of = one(*shards[0])
    for cut in shards[1:]:
        factor_of = factor_of * one(*cut)
    return factor_of


def deal_out(key, own, number, rows, number_of, top, reach, slope):
    ranking = jax.random.permutation(key, number_of)
    heavy_load, common = portions_of(number_of, rows * top, reach, slope, True), portions_of(number_of, rows * top, reach, slope, False)
    places = jnp.arange(number_of)

    def named(tallies, offset_by):
        used = int((tallies > 0).sum())
        fixed = max(1, used // 4)
        moved = fixed + (places - fixed + offset_by * (used - fixed)) % max(1, number_of - fixed)
        return jnp.zeros((number_of,), jnp.int32).at[ranking[jnp.where(places < fixed, places, moved)]].set(jnp.asarray(tallies, jnp.int32))

    tallies = jnp.where(number % 4 == 0, named(heavy_load, number // 4), named(common, number - number // 4 - 1))
    mixed = jax.random.permutation(jax.random.fold_in(own, 3), number_of)
    source_of, sink = mixed[0:number_of // 2 * 2:2], mixed[1:number_of // 2 * 2:2]
    slack = jnp.minimum(tallies[source_of] - 1, reach - tallies[sink]) // 2
    slack = jnp.where((source_of == ranking[0]) | (sink == ranking[0]) | (tallies[sink] == 0), 0, jnp.maximum(slack, 0))
    moved = jax.random.randint(jax.random.fold_in(own, 4), (number_of // 2,), 0, 1 << 20) % (slack + 1)
    tallies = tallies.at[source_of].add(-moved).at[sink].add(moved)
    labels = jnp.searchsorted(jnp.cumsum(tallies), jnp.arange(rows * top), side="right").astype(jnp.int32)
    table = labels.reshape(top, rows).T
    table = table[jax.random.permutation(jax.random.fold_in(own, 1), rows)]
    offset_by = jax.random.randint(jax.random.fold_in(own, 2), (rows, 1), 0, top)
    return jnp.take_along_axis(table, (jnp.arange(top)[None, :] + offset_by) % top, axis=1)


def portions_of(count, total, limit, skew, full):
    portions = [(1 << 20) // math.isqrt(rank ** skew) + 1 for rank in range(1, count + 1)]
    largest = limit if full else min(limit, max(-(-total // count), total * portions[0] // sum(portions)))
    least = 1 if total - largest >= count - 1 else 0
    counts, spare = [largest] + [least] * (count - 1), total - largest - least * (count - 1)
    while spare > 0:
        candidates = [i for i in range(1, count) if counts[i] < largest] or [i for i in range(1, count) if counts[i] < limit]
        mass, budget = sum([portions[i] for i in candidates]), spare
        for i in candidates:
            more = min(limit - counts[i], max(1, budget * portions[i] // mass), spare)
            counts[i] = counts[i] + more
            spare = spare - more
    return np.array(counts)


def noise(key, extent, spread, most, pieces=(), kind=jnp.bfloat16):
    drawn = jax.random.normal(key, extent, jnp.float32) * spread
    if len(pieces) > 0:
        drawn = levels(key, extent, pieces, -0.22, 0.18) * drawn
    return jnp.clip(drawn, min=-most, max=most).astype(kind)


def setup_inputs(seed: int = 0) -> dict:
    key_list = jax.random.split(jax.random.key(seed), 10)
    handoff = noise(key_list[0], (SEGMENTS, ROWS, D), 1.0, 6.0, ((0, 2), (1, 16)))
    saved_inputs = noise(key_list[1], (SEGMENTS, ROWS, D), 1.0, 6.0, ((0, 2), (1, 16)))
    cotangent = noise(key_list[2], (SEGMENTS, ROWS, D), 1.0, 6.0, ((0, 2), (1, 16)))
    ids_forward_keys = jax.random.split(jax.random.fold_in(key_list[3], 1), SEGMENTS * ROWS // ROWS_DEV)
    ids_forward_turns = jax.random.permutation(jax.random.fold_in(key_list[3], 3), SEGMENTS * ROWS // ROWS_DEV)
    ids_forward = jax.vmap(lambda own, number: deal_out(jax.random.fold_in(key_list[3], 2), own, number, ROWS_DEV, ALL_EXPERTS, 2, CAP, 2))(ids_forward_keys, ids_forward_turns).reshape((SEGMENTS, ROWS, 2))
    gates_forward = jnp.clip(0.25 + 0.75 * jax.random.uniform(key_list[4], (SEGMENTS, ROWS, 2), jnp.float32) ** levels(key_list[4], (SEGMENTS, ROWS, 2), ((0, 2), (1, 16)), -0.2, 0.2), 0.25, 1.0)
    ids_backward_keys = jax.random.split(jax.random.fold_in(key_list[5], 1), SEGMENTS * ROWS // ROWS_DEV)
    ids_backward_turns = jax.random.permutation(jax.random.fold_in(key_list[5], 3), SEGMENTS * ROWS // ROWS_DEV)
    ids_backward = jax.vmap(lambda own, number: deal_out(jax.random.fold_in(key_list[5], 2), own, number, ROWS_DEV, ALL_EXPERTS, 2, CAP, 2))(ids_backward_keys, ids_backward_turns).reshape((SEGMENTS, ROWS, 2))
    gates_backward = jnp.clip(0.25 + 0.75 * jax.random.uniform(key_list[6], (SEGMENTS, ROWS, 2), jnp.float32) ** levels(key_list[6], (SEGMENTS, ROWS, 2), ((0, 2), (1, 16)), -0.2, 0.2), 0.25, 1.0)
    weight_in = noise(key_list[7], (SEGMENTS, D, EXPERTS * FF), D ** -0.5, 0.09375, ((0, 2), (2, 16)))
    weight_out = noise(key_list[8], (SEGMENTS, EXPERTS * FF, D), FF ** -0.5, 0.125, ((0, 2), (1, 16)))
    return dict(handoff=handoff, saved_inputs=saved_inputs, cotangent=cotangent, ids_forward=ids_forward, gates_forward=gates_forward, ids_backward=ids_backward, gates_backward=gates_backward, weight_in=weight_in, weight_out=weight_out)


def slot_tables(expert_ids, gate_values, experts):
    row_count = expert_ids.shape[0]
    flat_ids = expert_ids.reshape(row_count * 2).astype(jnp.int32)
    window = jnp.arange(experts, dtype=jnp.int32)
    member = (flat_ids[None, :] == window[:, None]).astype(jnp.int32)
    before = jnp.cumsum(member, axis=1, dtype=jnp.int32) - member
    positions = jnp.arange(CAP, dtype=jnp.int32)
    picked_slots = (member[:, None, :] * (before[:, None, :] == positions[None, :, None]).astype(jnp.int32)).astype(jnp.float32)
    picked_slots = picked_slots.reshape(experts * CAP, row_count, 2)
    select = jnp.sum(picked_slots, axis=2)
    weighted = jnp.sum(picked_slots * gate_values[None, :, :].astype(jnp.float32), axis=2)
    return select, weighted


def expert_rows(group_args):
    row_block, in_weight, out_weight = group_args
    preact = jnp.dot(row_block, in_weight, preferred_element_type=jnp.float32)
    hidden = jax.nn.silu(preact).astype(jnp.bfloat16)
    hidden_width = in_weight.shape[1] // GROUP
    terms = jnp.einsum("rgh,ghd->rgd", hidden.reshape(-1, GROUP, hidden_width).astype(jnp.float32),
                       out_weight.reshape(GROUP, hidden_width, -1).astype(jnp.float32))
    rounded = lax.optimization_barrier(terms.astype(jnp.bfloat16))
    return jnp.sum(rounded.astype(jnp.float32), axis=1)


def expert_grads(group_args):
    row_block, grad_block, in_weight, out_weight = group_args
    preact = jnp.dot(row_block, in_weight, preferred_element_type=jnp.float32)
    sigmoid_v = jax.nn.sigmoid(preact)
    slope_v = sigmoid_v * (1.0 + preact * (1.0 - sigmoid_v))
    grad_hidden = jnp.dot(grad_block, out_weight.T, preferred_element_type=jnp.float32)
    grad_pre = (grad_hidden * slope_v).astype(jnp.bfloat16)
    hidden_width = in_weight.shape[1] // GROUP
    terms = jnp.einsum("rgh,ghd->rgd", grad_pre.reshape(-1, GROUP, hidden_width).astype(jnp.float32),
                       in_weight.T.reshape(GROUP, hidden_width, -1).astype(jnp.float32))
    rounded = lax.optimization_barrier(terms.astype(jnp.bfloat16))
    return jnp.sum(rounded.astype(jnp.float32), axis=1)


def one_segment(segment_args):
    inputs, saved_block, upstream, ids_f, gates_f, ids_b, gates_b, in_weight, out_weight = segment_args
    experts = N_EXPERT // GROUP
    sources = inputs.shape[0] // ROWS_DEV
    feature_width = inputs.shape[1]
    tables = jax.vmap(partial(slot_tables, experts=experts))
    highest = lax.Precision.HIGHEST
    in_experts = in_weight.reshape(feature_width, experts, FF).transpose(1, 0, 2)
    out_experts = out_weight.reshape(experts, FF, feature_width)

    select_f, weigh_f = tables(ids_f.reshape(sources, ROWS_DEV, 2), gates_f.reshape(sources, ROWS_DEV, 2))
    picked = jnp.einsum("sqr,srd->sqd", select_f, inputs.reshape(sources, ROWS_DEV, feature_width).astype(jnp.float32),
                        precision=highest).astype(jnp.bfloat16)
    by_expert = picked.reshape(sources, experts, CAP, feature_width).transpose(1, 0, 2, 3).reshape(experts, sources * CAP, feature_width)
    outputs = lax.map(expert_rows, (by_expert, in_experts, out_experts))
    outputs = outputs.reshape(experts, sources, CAP, feature_width).transpose(1, 0, 2, 3).reshape(sources, experts * CAP, feature_width)
    mixed = jnp.einsum("sqr,sqd->srd", weigh_f, outputs, precision=highest).astype(jnp.bfloat16).reshape(-1, feature_width)

    select_b, weigh_b = tables(ids_b.reshape(sources, ROWS_DEV, 2), gates_b.reshape(sources, ROWS_DEV, 2))
    rows_back = jnp.einsum("sqr,srd->sqd", select_b, saved_block.reshape(sources, ROWS_DEV, feature_width).astype(jnp.float32),
                           precision=highest).astype(jnp.bfloat16)
    grads_out = jnp.einsum("sqr,srd->sqd", weigh_b, upstream.reshape(sources, ROWS_DEV, feature_width).astype(jnp.float32),
                           precision=highest).astype(jnp.bfloat16)
    rows_expert = rows_back.reshape(sources, experts, CAP, feature_width).transpose(1, 0, 2, 3).reshape(experts, sources * CAP, feature_width)
    grads_expert = grads_out.reshape(sources, experts, CAP, feature_width).transpose(1, 0, 2, 3).reshape(experts, sources * CAP, feature_width)
    slot_grads = lax.map(expert_grads, (rows_expert, grads_expert, in_experts, out_experts))
    slot_grads = slot_grads.reshape(experts, sources, CAP, feature_width).transpose(1, 0, 2, 3).reshape(sources, experts * CAP, feature_width)
    grads = jnp.einsum("sqr,sqd->srd", select_b, slot_grads, precision=highest).astype(jnp.bfloat16).reshape(-1, feature_width)
    return mixed, grads


def reference(handoff, saved_inputs, cotangent, ids_forward, gates_forward, ids_backward, gates_backward, weight_in, weight_out):
    inputs = jnp.concatenate([handoff[:1], handoff[:-1]], axis=0)
    upstream = jnp.concatenate([cotangent[1:], cotangent[-1:]], axis=0)
    expert_mix, input_grads = lax.map(one_segment, (inputs, saved_inputs, upstream, ids_forward, gates_forward,
                                                   ids_backward, gates_backward, weight_in, weight_out))
    return expert_mix, input_grads
```

```python
import functools

import jax
import jax.numpy as jnp
from jax import lax
from jax.experimental import pallas as pl
from jax.experimental.pallas import tpu as pltpu
from jax.sharding import PartitionSpec as P

GROUP = 16
CAP = 5


def shifted(block, axis, distance):
    devices = range(lax.axis_size(axis))
    route = [(i - distance, i) for i in devices if i - distance in devices]
    return lax.ppermute(block, axis, route)


def slot_tables(expert_ids, gate_values, experts):
    row_count = expert_ids.shape[0]
    flat_ids = expert_ids.reshape(row_count * 2)
    window = jnp.arange(experts, dtype=jnp.int32)
    member = (flat_ids[None, :] == window[:, None]).astype(jnp.int32)
    before = jnp.cumsum(member, axis=1, dtype=jnp.int32) - member
    positions = jnp.arange(CAP, dtype=jnp.int32)
    picked_slots = (
        member[:, None, :] * (before[:, None, :] == positions[None, :, None]).astype(jnp.int32)
    ).astype(jnp.float32)
    picked_slots = picked_slots.reshape(experts * CAP, row_count, 2)
    select = jnp.sum(picked_slots, axis=2)
    weighted = jnp.sum(picked_slots * gate_values[None, :, :], axis=2)
    return (select, weighted)


def pack_direct(stacked, groups):
    stacks = stacked.shape[0]
    feature_width = stacked.shape[2]
    shaped = stacked.reshape(stacks, groups, 1, CAP, feature_width)
    spread_out = jnp.broadcast_to(shaped, (stacks, groups, GROUP, CAP, feature_width))
    return spread_out.reshape(stacks, groups * GROUP, CAP, feature_width)


def expert_forward(arriving, local_in, local_out):
    feature_width = arriving.shape[-1]
    preact = jnp.dot(
        arriving.reshape(-1, feature_width), local_in, preferred_element_type=jnp.float32
    )
    hidden = jax.nn.silu(preact).astype(jnp.bfloat16)
    partial_out = jnp.dot(hidden, local_out, preferred_element_type=jnp.float32).astype(
        jnp.bfloat16
    )
    return partial_out.reshape(arriving.shape)


def expert_backward(row_part, grad_part, local_in, local_out):
    feature_width = row_part.shape[-1]
    preact = jnp.dot(
        row_part.reshape(-1, feature_width), local_in, preferred_element_type=jnp.float32
    )
    sigmoid_v = jax.nn.sigmoid(preact)
    slope_v = sigmoid_v * (1.0 + preact * (1.0 - sigmoid_v))
    grad_hidden = jnp.einsum(
        "rd,hd->rh",
        grad_part.reshape(-1, feature_width),
        local_out,
        preferred_element_type=jnp.float32,
    )
    grad_pre = (grad_hidden * slope_v).astype(jnp.bfloat16)
    partial_grad = jnp.einsum(
        "rh,dh->rd", grad_pre, local_in, preferred_element_type=jnp.float32
    ).astype(jnp.bfloat16)
    return partial_grad.reshape(row_part.shape)


def gather_groups(returned, groups):
    feature_width = returned.shape[-1]
    summed = jnp.sum(
        returned.reshape(groups, GROUP, CAP, feature_width).astype(jnp.float32), axis=1
    )
    return summed.reshape(groups * CAP, feature_width)


def per_device(
    handoff,
    saved_inputs,
    cotangent,
    ids_forward,
    gates_forward,
    ids_backward,
    gates_backward,
    weight_in,
    weight_out,
):
    highest = lax.Precision.HIGHEST
    groups = lax.axis_size("expert") // GROUP
    segment_index = lax.axis_index("segment")
    last_segment = lax.axis_size("segment") - 1
    arrived = shifted(handoff, "segment", 1)
    inputs = jnp.where(segment_index == 0, handoff, arrived)[0]
    returned = shifted(cotangent, "segment", -1)
    upstream = jnp.where(segment_index == last_segment, cotangent, returned)[0]
    local_in = weight_in[0]
    local_out = weight_out[0]
    select_f, weigh_f = slot_tables(ids_forward[0], gates_forward[0], groups)
    picked = jnp.dot(
        select_f.astype(jnp.bfloat16), inputs, preferred_element_type=jnp.float32
    ).astype(jnp.bfloat16)
    select_b, weigh_b = slot_tables(ids_backward[0], gates_backward[0], groups)
    rows_back = jnp.dot(
        select_b.astype(jnp.bfloat16), saved_inputs[0], preferred_element_type=jnp.float32
    ).astype(jnp.bfloat16)
    grads_out = jnp.dot(
        weigh_b, upstream.astype(jnp.float32), precision=highest, preferred_element_type=jnp.float32
    ).astype(jnp.bfloat16)
    backward_stack = jnp.stack([rows_back, grads_out])
    arriving_f = lax.all_to_all(
        pack_direct(picked[None], groups), "expert", split_axis=1, concat_axis=1, tiled=True
    )
    arriving_b = lax.all_to_all(
        pack_direct(backward_stack, groups), "expert", split_axis=1, concat_axis=1, tiled=True
    )
    partial_f = expert_forward(arriving_f[0], local_in, local_out)
    back_f = lax.all_to_all(partial_f, "expert", split_axis=0, concat_axis=0, tiled=True)
    combined = gather_groups(back_f, groups)
    expert_mix = jnp.dot(
        weigh_f.T, combined, precision=highest, preferred_element_type=jnp.float32
    ).astype(jnp.bfloat16)
    partial_b = expert_backward(arriving_b[0], arriving_b[1], local_in, local_out)
    back_b = lax.all_to_all(partial_b, "expert", split_axis=0, concat_axis=0, tiled=True)
    slot_grads = gather_groups(back_b, groups)
    input_grads = jnp.dot(
        select_b.T, slot_grads, precision=highest, preferred_element_type=jnp.float32
    ).astype(jnp.bfloat16)
    return (expert_mix[None], input_grads[None])


MESH = pl.DeviceIdType.MESH
BLOCK = 16
THIRDS = 3
PARTS = 2
LANES = 128


def flipped(position, mask):
    bit = 1
    while bit <= mask:
        if mask & bit:
            position = position + bit * (1 - 2 * ((position // bit) % 2))
        bit *= 2
    return position


def exchange_kernel(
    planes,
    chunk,
    ids_f_hbm,
    gates_f_hbm,
    ids_b_hbm,
    gates_b_hbm,
    handoff,
    saved,
    cotangent,
    weight_in,
    weight_out,
    sums,
    places,
    gate_wide,
    rows_x,
    rows_s,
    w_first,
    w_second,
    blocks,
    req_send,
    req_recv,
    late_send,
    slope,
    y_send,
    y_keep,
    y_recv,
    z_send,
    z_recv,
    own_sum,
    ids_f,
    gates_f,
    ids_b,
    gates_b,
    local_sem,
    send_sem,
    recv_sem,
):
    segment = lax.axis_index("segment")
    expert = lax.axis_index("expert")
    row_count, width = rows_x.shape
    hidden = weight_out.shape[0]
    lengths = [min(chunk, width - q * chunk) for q in range(THIRDS)]

    def at_expert(mask):
        return {"expert": flipped(expert, mask)}

    def at_other(k):
        return {"segment": 1 - segment, "expert": flipped(expert, 4 * k)}

    sibling = at_expert(1)
    across = at_expert(2)
    mates = [None] + [at_expert(4 * k) for k in range(1, planes)]
    others = [at_other(k) for k in range(planes)]

    barrier = pltpu.get_barrier_semaphore()
    partners = mates[1:] + others + [across, sibling]
    for partner in partners:
        pl.semaphore_signal(barrier, inc=1, device_id=partner, device_id_type=MESH)

    tables = [
        pltpu.make_async_copy(source, target, local_sem.at[4 + i])
        for i, (source, target) in enumerate(
            [(ids_f_hbm, ids_f), (gates_f_hbm, gates_f), (ids_b_hbm, ids_b), (gates_b_hbm, gates_b)]
        )
    ]
    for table_copy in tables:
        table_copy.start()

    @pl.when(segment == 0)
    def _():
        pltpu.make_async_copy(handoff, rows_x, local_sem.at[0]).start()

    @pl.when(segment != 0)
    def _():
        pltpu.make_async_copy(cotangent, rows_x, local_sem.at[0]).start()

    load_x = pltpu.make_async_copy(handoff, rows_x, local_sem.at[0])
    load_s = pltpu.make_async_copy(saved, rows_s, local_sem.at[1])
    load_in = pltpu.make_async_copy(weight_in, w_first.at[0, :, 0:hidden], local_sem.at[2])
    load_out = pltpu.make_async_copy(weight_out, w_second.at[0, 0:hidden, :], local_sem.at[3])
    load_s.start()
    load_in.start()
    load_out.start()

    count = [0]
    started = []

    def remote(source, target, device):
        number = count[0]
        count[0] += 1
        return pltpu.make_async_remote_copy(
            src_ref=source,
            dst_ref=target,
            send_sem=send_sem.at[number],
            recv_sem=recv_sem.at[number],
            device_id=device,
            device_id_type=MESH,
        )

    def begin(copy):
        copy.start()
        started.append(copy)

    tiles = chunk // LANES
    edges = [tiles * i // PARTS * LANES for i in range(PARTS + 1)]
    parts = range(PARTS)
    cuts = [slice(low, high) for low, high in zip(edges[:-1], edges[1:])]

    def pieces(part):
        low, high = edges[part], edges[part + 1]
        middle = min(max(lengths[-1], low), high)
        return [
            (start, stop, THIRDS if stop <= lengths[-1] else THIRDS - 1)
            for start, stop in ((low, middle), (middle, high))
            if start < stop
        ]

    request = remote(req_send, req_recv, others[0])
    give_in = remote(weight_in, w_first.at[0, :, hidden : 2 * hidden], sibling)
    give_out = remote(weight_out, w_second.at[0, hidden : 2 * hidden, :], sibling)

    def ship(source, target, device):
        return [remote(source.at[:, cut], target.at[:, cut], device) for cut in cuts]

    gather_z = [
        [None] + [ship(blocks.at[kind, 0], blocks.at[kind, 2 * k], mates[k]) for k in range(1, planes)]
        for kind in range(2)
    ]
    gather_z.append([ship(late_send, blocks.at[2, 2 * k], others[k]) for k in range(planes)])
    gather_y = [
        [ship(blocks.at[kind, 2 * k], blocks.at[kind, 2 * k + 1], across) for k in range(planes)]
        for kind in range(3)
    ]
    reduce_y = [
        [ship(y_send.at[o, k], y_recv.at[o, k], across) for k in range(planes)] for o in range(2)
    ]
    reduce_z = [
        [None] + [ship(z_send.at[o, k], z_recv.at[o, k], mates[k]) for k in range(1, planes)]
        for o in range(2)
    ]

    for table_copy in tables:
        table_copy.wait()
    earlier = jnp.where(
        lax.broadcasted_iota(jnp.int32, (row_count, row_count), 0)
        < lax.broadcasted_iota(jnp.int32, (row_count, row_count), 1),
        1.0,
        0.0,
    ).astype(jnp.bfloat16)
    block_row = lax.broadcasted_iota(jnp.int32, (BLOCK, row_count), 0)
    third = sum((block_row >= CAP * q).astype(jnp.int32) for q in range(1, THIRDS + 1))
    slot = block_row - CAP * third

    def ranks(ids, gates):
        first, second = ids[0:1, :] == 0, ids[1:2, :] == 0
        member = jnp.where(first | second, 1.0, 0.0)
        gate = jnp.where(first, gates[0:1, :], 0.0) + jnp.where(second, gates[1:2, :], 0.0)
        wide = jnp.broadcast_to(member, (BLOCK, row_count))
        rank = jnp.dot(wide.astype(jnp.bfloat16), earlier, preferred_element_type=jnp.float32)
        placed = jnp.where((slot == rank.astype(jnp.int32)) & (third < THIRDS), wide, 0.0)
        return placed, gate

    placed_f, gate_f = ranks(ids_f, gates_f)
    placed_b, gate_b = ranks(ids_b, gates_b)
    later = (segment * jnp.ones((), jnp.int32)).astype(jnp.float32)
    scaled_b = placed_b * gate_b
    asked = scaled_b * (1.0 - later) + placed_f * later
    mine = placed_f * (1.0 - later) + scaled_b * later
    req_send[...] = jnp.concatenate([asked, jnp.zeros((BLOCK, LANES - row_count), jnp.float32)], axis=1)
    pl.semaphore_wait(barrier, len(partners))
    begin(request)

    def pick(weights, rows_ref, target):
        scale = jnp.sum(weights, axis=1, keepdims=True)
        choose = [
            jnp.where((weights != 0.0) & (third == q), 1.0, 0.0).astype(jnp.bfloat16) for q in range(THIRDS)
        ]
        for part in parts:
            for start, stop, thirds in pieces(part):
                total = sum(
                    jnp.dot(
                        choose[q],
                        rows_ref[:, q * chunk + start : q * chunk + stop],
                        preferred_element_type=jnp.float32,
                    )
                    for q in range(thirds)
                )
                target[:, start:stop] = (total * scale).astype(jnp.bfloat16)

    load_x.wait()
    pick(mine, rows_x, blocks.at[0, 0])
    for part in parts:
        begin(gather_y[0][0][part])
        for k in range(1, planes):
            begin(gather_z[0][k][part])
    load_s.wait()
    pick(placed_b, rows_s, blocks.at[1, 0])
    for part in parts:
        begin(gather_y[1][0][part])
        for k in range(1, planes):
            begin(gather_z[1][k][part])
    begin(give_in)
    begin(give_out)
    request.wait_recv()
    pick(req_recv[:, 0:row_count], rows_x, late_send)
    for part in parts:
        for k in range(planes):
            begin(gather_z[2][k][part])

    turn = 512 if width % 512 == 0 else LANES

    def transpose(low):
        half = slice(low, low + hidden)

        def step(number, carry):
            piece = pl.ds(pl.multiple_of(number * turn, turn), turn)
            w_first[1, piece, half] = w_second[0, half, piece].T
            w_second[1, half, piece] = w_first[0, piece, half].T
            return carry

        lax.fori_loop(0, width // turn, step, 0)

    def relay(kind, k):
        for part in parts:
            gather_z[kind][k][part].wait_recv()
            begin(gather_y[kind][k][part])

    load_in.wait()
    load_out.wait()
    transpose(0)
    for k in range(1, planes):
        relay(0, k)
    give_in.wait_recv()
    give_out.wait_recv()
    transpose(hidden)
    for k in range(1, planes):
        relay(1, k)
    unit = jnp.where(
        lax.broadcasted_iota(jnp.int32, (row_count, row_count), 0)
        == lax.broadcasted_iota(jnp.int32, (row_count, row_count), 1),
        1.0,
        0.0,
    )
    by_row = (((1,), (1,)), ((), ()))
    for i, placed in enumerate([placed_f, placed_b]):
        places[i] = lax.dot_general(
            unit.astype(jnp.bfloat16),
            placed.astype(jnp.bfloat16),
            by_row,
            preferred_element_type=jnp.float32,
        ).astype(jnp.bfloat16)
    gate_wide[...] = lax.dot_general(
        unit,
        jnp.broadcast_to(gate_f, (LANES, row_count)),
        by_row,
        precision=lax.Precision.HIGHEST,
        preferred_element_type=jnp.float32,
    )

    batch = 2 * planes * BLOCK
    place = lax.broadcasted_iota(jnp.int32, (batch, 2 * hidden), 0) % BLOCK

    def arrived(kind):
        for part in parts:
            for k in range(planes):
                gather_y[kind][k][part].wait_recv()

    def contract(kind, side):
        totals = [
            jnp.dot(
                blocks[kind, :, :, 0 : lengths[q]].reshape(batch, lengths[q]),
                w_first[side, q * chunk : q * chunk + lengths[q], :],
                preferred_element_type=jnp.float32,
            )
            for q in range(THIRDS)
        ]
        value = totals[0]
        for q in range(1, THIRDS):
            value = value + pltpu.roll(totals[q], batch - CAP * q, 0)
        return value

    def sigmoid(value):
        return 1.0 / (1.0 + jnp.exp(-value))

    order = [k for k in range(planes - 1, -1, -1)]

    def expand(value, side, o):
        value = jnp.where(place < CAP, value, 0.0)
        left = [pltpu.roll(value, CAP * q, 0).astype(jnp.bfloat16) if q else value.astype(jnp.bfloat16) for q in range(THIRDS)]
        for part in parts:
            for start, stop, thirds in pieces(part):
                total = sum(
                    jnp.dot(
                        left[q],
                        w_second[side, :, q * chunk + start : q * chunk + stop],
                        preferred_element_type=jnp.float32,
                    )
                    for q in range(thirds)
                ).reshape(planes, 2, BLOCK, stop - start)
                y_keep[o, :, :, start:stop] = total[:, 0]
                y_send[o, :, :, start:stop] = total[:, 1].astype(jnp.bfloat16)
            for k in order:
                begin(reduce_y[o][k][part])

    def join(o, part):
        cut = cuts[part]
        for k in order:
            reduce_y[o][k][part].wait_recv()
            total = y_keep[o, k, :, cut] + y_recv[o, k, :, cut].astype(jnp.float32)
            if k == 0:
                own_sum[o, :, cut] = total
            else:
                z_send[o, k, :, cut] = total.astype(jnp.bfloat16)
                begin(reduce_z[o][k][part])

    relay(2, 0)
    arrived(0)
    first = contract(0, segment)
    relay(2, 1)
    arrived(1)
    pre = contract(1, 0)
    gate = sigmoid(pre)
    slope[...] = gate * (1.0 + pre * (1.0 - gate))
    expand(first * sigmoid(first) * (1.0 - later) + first * slope[...] * later, segment, 0)
    for k in range(2, planes):
        relay(2, k)
    arrived(2)
    last = contract(2, 1 - segment)
    expand(last * slope[...] * (1.0 - later) + last * sigmoid(last) * later, 1 - segment, 1)
    for o in range(2):
        for part in parts:
            join(o, part)
    for o in range(2):
        total = own_sum[o]
        for k in range(1, planes):
            for part in parts:
                reduce_z[o][k][part].wait_recv()
            total = total + z_recv[o, k].astype(jnp.float32)
        sums[segment if o == 0 else 1 - segment] = total.astype(jnp.bfloat16)
    for copy in started:
        copy.wait_send()


def scatter_kernel(chunk, sums, places, gate_wide, out_f, out_b):
    width = out_f.shape[1]
    column = lax.broadcasted_iota(jnp.int32, places.shape[1:], 1)
    gate = gate_wide[:, 0:1]
    for q in range(THIRDS):
        low, high = q * chunk, min((q + 1) * chunk, width)
        inside = (column >= CAP * q) & (column < CAP * (q + 1))
        for i, out in enumerate([out_f, out_b]):
            value = jnp.dot(
                jnp.where(inside, places[i], 0.0).astype(jnp.bfloat16),
                sums[i, :, 0 : high - low],
                preferred_element_type=jnp.float32,
            )
            out[:, low:high] = (value * gate if i == 0 else value).astype(jnp.bfloat16)


def exchange(planes, handoff, saved_inputs, cotangent, ids_forward, gates_forward, ids_backward, gates_backward, weight_in, weight_out):
    rows, width = handoff.shape[1:]
    hidden = weight_out.shape[1]
    chunk = -(-(width // LANES) // THIRDS) * LANES
    bf16, f32 = jnp.bfloat16, jnp.float32
    copies = 3 + PARTS * (2 * (2 * planes - 1) + 2 * planes + 2 * (2 * planes - 1))
    vmem = pl.BlockSpec(memory_space=pltpu.VMEM)
    hbm = pl.BlockSpec(memory_space=pl.ANY)
    sums, places, gate_wide = pl.pallas_call(
        functools.partial(exchange_kernel, planes, chunk),
        out_shape=[
            jax.ShapeDtypeStruct((2, BLOCK, chunk), bf16),
            jax.ShapeDtypeStruct((2, rows, BLOCK), bf16),
            jax.ShapeDtypeStruct((rows, LANES), f32),
        ],
        in_specs=[hbm] * 9,
        out_specs=[vmem] * 3,
        scratch_shapes=[
            pltpu.VMEM((rows, width), bf16),
            pltpu.VMEM((rows, width), bf16),
            pltpu.VMEM((2, width, 2 * hidden), bf16),
            pltpu.VMEM((2, 2 * hidden, width), bf16),
            pltpu.VMEM((3, 2 * planes, BLOCK, chunk), bf16),
            pltpu.VMEM((BLOCK, LANES), f32),
            pltpu.VMEM((BLOCK, LANES), f32),
            pltpu.VMEM((BLOCK, chunk), bf16),
            pltpu.VMEM((2 * planes * BLOCK, 2 * hidden), f32),
            pltpu.VMEM((2, planes, BLOCK, chunk), bf16),
            pltpu.VMEM((2, planes, BLOCK, chunk), f32),
            pltpu.VMEM((2, planes, BLOCK, chunk), bf16),
            pltpu.VMEM((2, planes, BLOCK, chunk), bf16),
            pltpu.VMEM((2, planes, BLOCK, chunk), bf16),
            pltpu.VMEM((2, BLOCK, chunk), f32),
            pltpu.VMEM((2, rows), jnp.int32),
            pltpu.VMEM((2, rows), f32),
            pltpu.VMEM((2, rows), jnp.int32),
            pltpu.VMEM((2, rows), f32),
            pltpu.SemaphoreType.DMA((8,)),
            pltpu.SemaphoreType.DMA((copies,)),
            pltpu.SemaphoreType.DMA((copies,)),
        ],
        compiler_params=pltpu.CompilerParams(
            collective_id=0, has_side_effects=True
        ),
    )(
        ids_forward[0].T,
        gates_forward[0].T,
        ids_backward[0].T,
        gates_backward[0].T,
        handoff[0],
        saved_inputs[0],
        cotangent[0],
        weight_in[0],
        weight_out[0],
    )
    mixed, grads = pl.pallas_call(
        functools.partial(scatter_kernel, chunk),
        out_shape=[jax.ShapeDtypeStruct((rows, width), bf16)] * 2,
        in_specs=[vmem] * 3,
        out_specs=[vmem] * 2,
    )(sums, places, gate_wide)
    return (mixed[None], grads[None])


def device_body(mesh):
    segments, experts = mesh.shape["segment"], mesh.shape["expert"]
    planes = experts // 4
    if segments == 2 and experts == GROUP and planes & (planes - 1) == 0:
        return functools.partial(exchange, planes)
    return per_device


def solution(mesh):
    return jax.shard_map(
        device_body(mesh),
        mesh=mesh,
        in_specs=(
            P("segment", "expert", None),
            P("segment", "expert", None),
            P("segment", "expert", None),
            P("segment", "expert", None),
            P("segment", "expert", None),
            P("segment", "expert", None),
            P("segment", "expert", None),
            P("segment", None, "expert"),
            P("segment", "expert", None),
        ),
        out_specs=(P("segment", "expert", None), P("segment", "expert", None)),
        check_vma=False,
    )
```

```python
import functools

import jax
import jax.numpy as jnp
from jax import lax
from jax.experimental import pallas as pl
from jax.experimental.pallas import tpu as pltpu
from jax.sharding import PartitionSpec as P

GROUP = 16
CAP = 5


def shifted(block, axis, distance):
    devices = range(lax.axis_size(axis))
    route = [(i - distance, i) for i in devices if i - distance in devices]
    return lax.ppermute(block, axis, route)


def slot_tables(expert_ids, gate_values, experts):
    row_count = expert_ids.shape[0]
    flat_ids = expert_ids.reshape(row_count * 2)
    window = jnp.arange(experts, dtype=jnp.int32)
    member = (flat_ids[None, :] == window[:, None]).astype(jnp.int32)
    before = jnp.cumsum(member, axis=1, dtype=jnp.int32) - member
    positions = jnp.arange(CAP, dtype=jnp.int32)
    picked_slots = (
        member[:, None, :] * (before[:, None, :] == positions[None, :, None]).astype(jnp.int32)
    ).astype(jnp.float32)
    picked_slots = picked_slots.reshape(experts * CAP, row_count, 2)
    select = jnp.sum(picked_slots, axis=2)
    weighted = jnp.sum(picked_slots * gate_values[None, :, :], axis=2)
    return (select, weighted)


def pack_direct(stacked, groups):
    stacks = stacked.shape[0]
    feature_width = stacked.shape[2]
    shaped = stacked.reshape(stacks, groups, 1, CAP, feature_width)
    spread_out = jnp.broadcast_to(shaped, (stacks, groups, GROUP, CAP, feature_width))
    return spread_out.reshape(stacks, groups * GROUP, CAP, feature_width)


def expert_forward(arriving, local_in, local_out):
    feature_width = arriving.shape[-1]
    preact = jnp.dot(
        arriving.reshape(-1, feature_width), local_in, preferred_element_type=jnp.float32
    )
    hidden = jax.nn.silu(preact).astype(jnp.bfloat16)
    partial_out = jnp.dot(hidden, local_out, preferred_element_type=jnp.float32).astype(
        jnp.bfloat16
    )
    return partial_out.reshape(arriving.shape)


def expert_backward(row_part, grad_part, local_in, local_out):
    feature_width = row_part.shape[-1]
    preact = jnp.dot(
        row_part.reshape(-1, feature_width), local_in, preferred_element_type=jnp.float32
    )
    sigmoid_v = jax.nn.sigmoid(preact)
    slope_v = sigmoid_v * (1.0 + preact * (1.0 - sigmoid_v))
    grad_hidden = jnp.einsum(
        "rd,hd->rh",
        grad_part.reshape(-1, feature_width),
        local_out,
        preferred_element_type=jnp.float32,
    )
    grad_pre = (grad_hidden * slope_v).astype(jnp.bfloat16)
    partial_grad = jnp.einsum(
        "rh,dh->rd", grad_pre, local_in, preferred_element_type=jnp.float32
    ).astype(jnp.bfloat16)
    return partial_grad.reshape(row_part.shape)


def gather_groups(returned, groups):
    feature_width = returned.shape[-1]
    summed = jnp.sum(
        returned.reshape(groups, GROUP, CAP, feature_width).astype(jnp.float32), axis=1
    )
    return summed.reshape(groups * CAP, feature_width)


def per_device(
    handoff,
    saved_inputs,
    cotangent,
    ids_forward,
    gates_forward,
    ids_backward,
    gates_backward,
    weight_in,
    weight_out,
):
    highest = lax.Precision.HIGHEST
    groups = lax.axis_size("expert") // GROUP
    segment_index = lax.axis_index("segment")
    last_segment = lax.axis_size("segment") - 1
    arrived = shifted(handoff, "segment", 1)
    inputs = jnp.where(segment_index == 0, handoff, arrived)[0]
    returned = shifted(cotangent, "segment", -1)
    upstream = jnp.where(segment_index == last_segment, cotangent, returned)[0]
    local_in = weight_in[0]
    local_out = weight_out[0]
    select_f, weigh_f = slot_tables(ids_forward[0], gates_forward[0], groups)
    picked = jnp.dot(
        select_f.astype(jnp.bfloat16), inputs, preferred_element_type=jnp.float32
    ).astype(jnp.bfloat16)
    select_b, weigh_b = slot_tables(ids_backward[0], gates_backward[0], groups)
    rows_back = jnp.dot(
        select_b.astype(jnp.bfloat16), saved_inputs[0], preferred_element_type=jnp.float32
    ).astype(jnp.bfloat16)
    grads_out = jnp.dot(
        weigh_b, upstream.astype(jnp.float32), precision=highest, preferred_element_type=jnp.float32
    ).astype(jnp.bfloat16)
    backward_stack = jnp.stack([rows_back, grads_out])
    arriving_f = lax.all_to_all(
        pack_direct(picked[None], groups), "expert", split_axis=1, concat_axis=1, tiled=True
    )
    arriving_b = lax.all_to_all(
        pack_direct(backward_stack, groups), "expert", split_axis=1, concat_axis=1, tiled=True
    )
    partial_f = expert_forward(arriving_f[0], local_in, local_out)
    back_f = lax.all_to_all(partial_f, "expert", split_axis=0, concat_axis=0, tiled=True)
    combined = gather_groups(back_f, groups)
    expert_mix = jnp.dot(
        weigh_f.T, combined, precision=highest, preferred_element_type=jnp.float32
    ).astype(jnp.bfloat16)
    partial_b = expert_backward(arriving_b[0], arriving_b[1], local_in, local_out)
    back_b = lax.all_to_all(partial_b, "expert", split_axis=0, concat_axis=0, tiled=True)
    slot_grads = gather_groups(back_b, groups)
    input_grads = jnp.dot(
        select_b.T, slot_grads, precision=highest, preferred_element_type=jnp.float32
    ).astype(jnp.bfloat16)
    return (expert_mix[None], input_grads[None])


MESH = pl.DeviceIdType.MESH
BLOCK = 16
THIRDS = 3
PARTS = 2
LANES = 128


def flipped(position, mask):
    bit = 1
    while bit <= mask:
        if mask & bit:
            position = position + bit * (1 - 2 * ((position // bit) % 2))
        bit *= 2
    return position


def exchange_kernel(
    planes,
    chunk,
    ids_f_hbm,
    gates_f_hbm,
    ids_b_hbm,
    gates_b_hbm,
    handoff,
    saved,
    cotangent,
    weight_in,
    weight_out,
    sums,
    places,
    gate_wide,
    rows_x,
    rows_s,
    w_first,
    w_second,
    blocks,
    req_send,
    req_recv,
    late_send,
    slope,
    y_send,
    y_keep,
    y_recv,
    z_send,
    z_recv,
    own_sum,
    ids_f,
    gates_f,
    ids_b,
    gates_b,
    local_sem,
    send_sem,
    recv_sem,
):
    segment = lax.axis_index("segment")
    expert = lax.axis_index("expert")
    row_count, width = rows_x.shape
    hidden = weight_out.shape[0]
    lengths = [min(chunk, width - q * chunk) for q in range(THIRDS)]

    def at_expert(mask):
        return {"expert": flipped(expert, mask)}

    def at_other(k):
        return {"segment": 1 - segment, "expert": flipped(expert, 4 * k)}

    sibling = at_expert(1)
    across = at_expert(2)
    mates = [None] + [at_expert(4 * k) for k in range(1, planes)]
    others = [at_other(k) for k in range(planes)]

    barrier = pltpu.get_barrier_semaphore()
    partners = mates[1:] + others + [across, sibling]
    for partner in partners:
        pl.semaphore_signal(barrier, inc=1, device_id=partner, device_id_type=MESH)

    tables = [
        pltpu.make_async_copy(source, target, local_sem.at[4 + i])
        for i, (source, target) in enumerate(
            [(ids_f_hbm, ids_f), (gates_f_hbm, gates_f), (ids_b_hbm, ids_b), (gates_b_hbm, gates_b)]
        )
    ]
    for table_copy in tables:
        table_copy.start()

    @pl.when(segment == 0)
    def _():
        pltpu.make_async_copy(handoff, rows_x, local_sem.at[0]).start()

    @pl.when(segment != 0)
    def _():
        pltpu.make_async_copy(cotangent, rows_x, local_sem.at[0]).start()

    load_x = pltpu.make_async_copy(handoff, rows_x, local_sem.at[0])
    load_s = pltpu.make_async_copy(saved, rows_s, local_sem.at[1])
    load_in = pltpu.make_async_copy(weight_in, w_first.at[0, :, 0:hidden], local_sem.at[2])
    load_out = pltpu.make_async_copy(weight_out, w_second.at[0, 0:hidden, :], local_sem.at[3])
    load_s.start()
    load_in.start()
    load_out.start()

    count = [0]
    started = []
    started_inner = []

    def remote(source, target, device, landing=None):
        number = count[0]
        count[0] += 1
        return pltpu.make_async_remote_copy(
            src_ref=source,
            dst_ref=target,
            send_sem=send_sem.at[number],
            recv_sem=recv_sem.at[number if landing is None else landing],
            device_id=device,
            device_id_type=MESH,
        )

    def begin(copy):
        copy.start()
        started.append(copy)

    plane = expert // 4
    inner = (plane > 0) & (plane < planes - 1)

    def begin_inner(copies):
        @pl.when(inner)
        def _():
            for copy in copies:
                copy.start()

        started_inner.extend(copies)

    tiles = chunk // LANES
    edges = [tiles * i // PARTS * LANES for i in range(PARTS + 1)]
    parts = range(PARTS)
    cuts = [slice(low, high) for low, high in zip(edges[:-1], edges[1:])]

    def pieces(part):
        low, high = edges[part], edges[part + 1]
        middle = min(max(lengths[-1], low), high)
        return [
            (start, stop, THIRDS if stop <= lengths[-1] else THIRDS - 1)
            for start, stop in ((low, middle), (middle, high))
            if start < stop
        ]

    request = remote(req_send, req_recv, others[0])
    give_in = remote(weight_in, w_first.at[0, :, hidden : 2 * hidden], sibling)
    give_out = remote(weight_out, w_second.at[0, hidden : 2 * hidden, :], sibling)

    def ship(source, target, device, landing=None):
        return [
            remote(source.at[:, cut], target.at[:, cut], device, None if landing is None else landing + part)
            for part, cut in enumerate(cuts)
        ]

    gather_z = []
    first_number = []
    for kind in range(2):
        gather_z.append(
            [None] + [ship(blocks.at[kind, 0], blocks.at[kind, 2 * k], mates[k]) for k in range(1, planes)]
        )
        first_number.append(count[0] - PARTS)
    gather_z.append([ship(late_send, blocks.at[2, 2 * k], others[k]) for k in range(planes)])
    first_number.append(count[0] - PARTS)
    far = planes - 1
    forward_z = [
        ship(blocks.at[kind, 4], blocks.at[kind, 2 * far], mates[1], first_number[kind]) for kind in range(3)
    ]
    gather_y = [
        [ship(blocks.at[kind, 2 * k], blocks.at[kind, 2 * k + 1], across) for k in range(planes)]
        for kind in range(3)
    ]
    reduce_y = [
        [ship(y_send.at[o, k], y_recv.at[o, k], across) for k in range(planes)] for o in range(2)
    ]
    reduce_z = [
        [None] + [ship(z_send.at[o, k], z_recv.at[o, k], mates[k]) for k in range(1, planes)]
        for o in range(2)
    ]

    for table_copy in tables:
        table_copy.wait()
    earlier = jnp.where(
        lax.broadcasted_iota(jnp.int32, (row_count, row_count), 0)
        < lax.broadcasted_iota(jnp.int32, (row_count, row_count), 1),
        1.0,
        0.0,
    ).astype(jnp.bfloat16)
    block_row = lax.broadcasted_iota(jnp.int32, (BLOCK, row_count), 0)
    third = sum((block_row >= CAP * q).astype(jnp.int32) for q in range(1, THIRDS + 1))
    slot = block_row - CAP * third

    def ranks(ids, gates):
        first, second = ids[0:1, :] == 0, ids[1:2, :] == 0
        member = jnp.where(first | second, 1.0, 0.0)
        gate = jnp.where(first, gates[0:1, :], 0.0) + jnp.where(second, gates[1:2, :], 0.0)
        wide = jnp.broadcast_to(member, (BLOCK, row_count))
        rank = jnp.dot(wide.astype(jnp.bfloat16), earlier, preferred_element_type=jnp.float32)
        placed = jnp.where((slot == rank.astype(jnp.int32)) & (third < THIRDS), wide, 0.0)
        return placed, gate

    placed_f, gate_f = ranks(ids_f, gates_f)
    placed_b, gate_b = ranks(ids_b, gates_b)
    later = (segment * jnp.ones((), jnp.int32)).astype(jnp.float32)
    scaled_b = placed_b * gate_b
    asked = scaled_b * (1.0 - later) + placed_f * later
    mine = placed_f * (1.0 - later) + scaled_b * later
    req_send[...] = jnp.concatenate([asked, jnp.zeros((BLOCK, LANES - row_count), jnp.float32)], axis=1)
    pl.semaphore_wait(barrier, len(partners))
    begin(request)

    def pick(weights, rows_ref, target):
        scale = jnp.sum(weights, axis=1, keepdims=True)
        choose = [
            jnp.where((weights != 0.0) & (third == q), 1.0, 0.0).astype(jnp.bfloat16) for q in range(THIRDS)
        ]
        for part in parts:
            for start, stop, thirds in pieces(part):
                total = sum(
                    jnp.dot(
                        choose[q],
                        rows_ref[:, q * chunk + start : q * chunk + stop],
                        preferred_element_type=jnp.float32,
                    )
                    for q in range(thirds)
                )
                target[:, start:stop] = (total * scale).astype(jnp.bfloat16)

    def spread(kind):
        for part in parts:
            begin(gather_y[kind][0][part])
            for k in range(1, far):
                begin(gather_z[kind][k][part])
        begin_inner(gather_z[kind][far])

    load_x.wait()
    pick(mine, rows_x, blocks.at[0, 0])
    spread(0)
    load_s.wait()
    pick(placed_b, rows_s, blocks.at[1, 0])
    spread(1)
    begin(give_in)
    begin(give_out)
    request.wait_recv()
    pick(req_recv[:, 0:row_count], rows_x, late_send)
    for part in parts:
        for k in range(far):
            begin(gather_z[2][k][part])
    begin_inner(gather_z[2][far])

    turn = 512 if width % 512 == 0 else LANES

    def transpose(low, share=0, shares=1):
        half = slice(low, low + hidden)

        def step(number, carry):
            piece = pl.ds(pl.multiple_of(number * turn, turn), turn)
            w_first[1, piece, half] = w_second[0, half, piece].T
            w_second[1, half, piece] = w_first[0, piece, half].T
            return carry

        steps = width // turn
        lax.fori_loop(steps * share // shares, steps * (share + 1) // shares, step, 0)

    def relay(kind, k):
        for part in parts:
            gather_z[kind][k][part].wait_recv()
            begin(gather_y[kind][k][part])
            if k == 2:
                begin_inner([forward_z[kind][part]])

    load_in.wait()
    load_out.wait()
    transpose(0)
    relay(0, 1)
    relay(0, 2)
    give_in.wait_recv()
    give_out.wait_recv()
    transpose(hidden, 0, 4)
    relay(1, 1)
    transpose(hidden, 1, 4)
    relay(1, 2)
    relay(2, 0)
    transpose(hidden, 2, 4)
    relay(0, far)
    transpose(hidden, 3, 4)
    relay(1, far)
    relay(2, 1)
    unit = jnp.where(
        lax.broadcasted_iota(jnp.int32, (row_count, row_count), 0)
        == lax.broadcasted_iota(jnp.int32, (row_count, row_count), 1),
        1.0,
        0.0,
    )
    by_row = (((1,), (1,)), ((), ()))
    for i, placed in enumerate([placed_f, placed_b]):
        places[i] = lax.dot_general(
            unit.astype(jnp.bfloat16),
            placed.astype(jnp.bfloat16),
            by_row,
            preferred_element_type=jnp.float32,
        ).astype(jnp.bfloat16)
    gate_wide[...] = lax.dot_general(
        unit,
        jnp.broadcast_to(gate_f, (LANES, row_count)),
        by_row,
        precision=lax.Precision.HIGHEST,
        preferred_element_type=jnp.float32,
    )

    batch = 2 * planes * BLOCK
    place = lax.broadcasted_iota(jnp.int32, (batch, 2 * hidden), 0) % BLOCK

    def arrived(kind):
        for part in parts:
            for k in range(planes):
                gather_y[kind][k][part].wait_recv()

    def contract(kind, side):
        totals = [
            jnp.dot(
                blocks[kind, :, :, 0 : lengths[q]].reshape(batch, lengths[q]),
                w_first[side, q * chunk : q * chunk + lengths[q], :],
                preferred_element_type=jnp.float32,
            )
            for q in range(THIRDS)
        ]
        value = totals[0]
        for q in range(1, THIRDS):
            value = value + pltpu.roll(totals[q], batch - CAP * q, 0)
        return value

    def sigmoid(value):
        return 1.0 / (1.0 + jnp.exp(-value))

    order = [k for k in range(planes - 1, -1, -1)]

    def expand(value, side, o):
        value = jnp.where(place < CAP, value, 0.0)
        left = [pltpu.roll(value, CAP * q, 0).astype(jnp.bfloat16) if q else value.astype(jnp.bfloat16) for q in range(THIRDS)]
        for part in parts:
            for start, stop, thirds in pieces(part):
                total = sum(
                    jnp.dot(
                        left[q],
                        w_second[side, :, q * chunk + start : q * chunk + stop],
                        preferred_element_type=jnp.float32,
                    )
                    for q in range(thirds)
                ).reshape(planes, 2, BLOCK, stop - start)
                y_keep[o, :, :, start:stop] = total[:, 0]
                y_send[o, :, :, start:stop] = total[:, 1].astype(jnp.bfloat16)
            for k in order:
                begin(reduce_y[o][k][part])

    def join(o, part):
        cut = cuts[part]
        for k in order:
            reduce_y[o][k][part].wait_recv()
            total = y_keep[o, k, :, cut] + y_recv[o, k, :, cut].astype(jnp.float32)
            if k == 0:
                own_sum[o, :, cut] = total
            else:
                z_send[o, k, :, cut] = total.astype(jnp.bfloat16)
                begin(reduce_z[o][k][part])

    relay(2, 2)
    arrived(0)
    first = contract(0, segment)
    relay(2, far)
    arrived(1)
    pre = contract(1, 0)
    gate = sigmoid(pre)
    slope[...] = gate * (1.0 + pre * (1.0 - gate))
    expand(first * sigmoid(first) * (1.0 - later) + first * slope[...] * later, segment, 0)
    arrived(2)
    last = contract(2, 1 - segment)
    expand(last * slope[...] * (1.0 - later) + last * sigmoid(last) * later, 1 - segment, 1)
    for o in range(2):
        for part in parts:
            join(o, part)
    for o in range(2):
        total = own_sum[o]
        for k in range(1, planes):
            for part in parts:
                reduce_z[o][k][part].wait_recv()
            total = total + z_recv[o, k].astype(jnp.float32)
        sums[segment if o == 0 else 1 - segment] = total.astype(jnp.bfloat16)
    for copy in started:
        copy.wait_send()

    @pl.when(inner)
    def _():
        for copy in started_inner:
            copy.wait_send()


def scatter_kernel(chunk, sums, places, gate_wide, out_f, out_b):
    width = out_f.shape[1]
    column = lax.broadcasted_iota(jnp.int32, places.shape[1:], 1)
    gate = gate_wide[:, 0:1]
    for q in range(THIRDS):
        low, high = q * chunk, min((q + 1) * chunk, width)
        inside = (column >= CAP * q) & (column < CAP * (q + 1))
        for i, out in enumerate([out_f, out_b]):
            value = jnp.dot(
                jnp.where(inside, places[i], 0.0).astype(jnp.bfloat16),
                sums[i, :, 0 : high - low],
                preferred_element_type=jnp.float32,
            )
            out[:, low:high] = (value * gate if i == 0 else value).astype(jnp.bfloat16)


def exchange(planes, handoff, saved_inputs, cotangent, ids_forward, gates_forward, ids_backward, gates_backward, weight_in, weight_out):
    rows, width = handoff.shape[1:]
    hidden = weight_out.shape[1]
    chunk = -(-(width // LANES) // THIRDS) * LANES
    bf16, f32 = jnp.bfloat16, jnp.float32
    copies = 3 + PARTS * (2 * (2 * planes - 1) + 2 * planes + 3 + 2 * (2 * planes - 1))
    vmem = pl.BlockSpec(memory_space=pltpu.VMEM)
    hbm = pl.BlockSpec(memory_space=pl.ANY)
    sums, places, gate_wide = pl.pallas_call(
        functools.partial(exchange_kernel, planes, chunk),
        out_shape=[
            pltpu.VMEM((2, BLOCK, chunk), bf16),
            pltpu.VMEM((2, rows, BLOCK), bf16),
            pltpu.VMEM((rows, LANES), f32),
        ],
        in_specs=[hbm] * 9,
        out_specs=[vmem] * 3,
        scratch_shapes=[
            pltpu.VMEM((rows, width), bf16),
            pltpu.VMEM((rows, width), bf16),
            pltpu.VMEM((2, width, 2 * hidden), bf16),
            pltpu.VMEM((2, 2 * hidden, width), bf16),
            pltpu.VMEM((3, 2 * planes, BLOCK, chunk), bf16),
            pltpu.VMEM((BLOCK, LANES), f32),
            pltpu.VMEM((BLOCK, LANES), f32),
            pltpu.VMEM((BLOCK, chunk), bf16),
            pltpu.VMEM((2 * planes * BLOCK, 2 * hidden), f32),
            pltpu.VMEM((2, planes, BLOCK, chunk), bf16),
            pltpu.VMEM((2, planes, BLOCK, chunk), f32),
            pltpu.VMEM((2, planes, BLOCK, chunk), bf16),
            pltpu.VMEM((2, planes, BLOCK, chunk), bf16),
            pltpu.VMEM((2, planes, BLOCK, chunk), bf16),
            pltpu.VMEM((2, BLOCK, chunk), f32),
            pltpu.VMEM((2, rows), jnp.int32),
            pltpu.VMEM((2, rows), f32),
            pltpu.VMEM((2, rows), jnp.int32),
            pltpu.VMEM((2, rows), f32),
            pltpu.SemaphoreType.DMA((8,)),
            pltpu.SemaphoreType.DMA((copies,)),
            pltpu.SemaphoreType.DMA((copies,)),
        ],
        compiler_params=pltpu.CompilerParams(
            collective_id=0, has_side_effects=True
        ),
    )(
        ids_forward[0].T,
        gates_forward[0].T,
        ids_backward[0].T,
        gates_backward[0].T,
        handoff[0],
        saved_inputs[0],
        cotangent[0],
        weight_in[0],
        weight_out[0],
    )
    mixed, grads = pl.pallas_call(
        functools.partial(scatter_kernel, chunk),
        out_shape=[jax.ShapeDtypeStruct((rows, width), bf16)] * 2,
        in_specs=[vmem] * 3,
        out_specs=[vmem] * 2,
    )(*[pltpu.with_memory_space_constraint(x, pltpu.VMEM) for x in (sums, places, gate_wide)])
    return (mixed[None], grads[None])


def device_body(mesh):
    segments, experts = mesh.shape["segment"], mesh.shape["expert"]
    planes = experts // 4
    if segments == 2 and experts == GROUP and planes == 4:
        return functools.partial(exchange, planes)
    return per_device


def solution(mesh):
    return jax.shard_map(
        device_body(mesh),
        mesh=mesh,
        in_specs=(
            P("segment", "expert", None),
            P("segment", "expert", None),
            P("segment", "expert", None),
            P("segment", "expert", None),
            P("segment", "expert", None),
            P("segment", "expert", None),
            P("segment", "expert", None),
            P("segment", None, "expert"),
            P("segment", "expert", None),
        ),
        out_specs=(P("segment", "expert", None), P("segment", "expert", None)),
        check_vma=False,
    )
```

```python
import functools

import jax
import jax.numpy as jnp
from jax import lax
from jax.experimental import pallas as pl
from jax.experimental.pallas import tpu as pltpu
from jax.sharding import PartitionSpec as P

GROUP = 16
CAP = 5


def shifted(block, axis, distance):
    devices = range(lax.axis_size(axis))
    route = [(i - distance, i) for i in devices if i - distance in devices]
    return lax.ppermute(block, axis, route)


def slot_tables(expert_ids, gate_values, experts):
    row_count = expert_ids.shape[0]
    flat_ids = expert_ids.reshape(row_count * 2)
    window = jnp.arange(experts, dtype=jnp.int32)
    member = (flat_ids[None, :] == window[:, None]).astype(jnp.int32)
    before = jnp.cumsum(member, axis=1, dtype=jnp.int32) - member
    positions = jnp.arange(CAP, dtype=jnp.int32)
    picked_slots = (
        member[:, None, :] * (before[:, None, :] == positions[None, :, None]).astype(jnp.int32)
    ).astype(jnp.float32)
    picked_slots = picked_slots.reshape(experts * CAP, row_count, 2)
    select = jnp.sum(picked_slots, axis=2)
    weighted = jnp.sum(picked_slots * gate_values[None, :, :], axis=2)
    return (select, weighted)


def pack_direct(stacked, groups):
    stacks = stacked.shape[0]
    feature_width = stacked.shape[2]
    shaped = stacked.reshape(stacks, groups, 1, CAP, feature_width)
    spread_out = jnp.broadcast_to(shaped, (stacks, groups, GROUP, CAP, feature_width))
    return spread_out.reshape(stacks, groups * GROUP, CAP, feature_width)


def expert_forward(arriving, local_in, local_out):
    feature_width = arriving.shape[-1]
    preact = jnp.dot(
        arriving.reshape(-1, feature_width), local_in, preferred_element_type=jnp.float32
    )
    hidden = jax.nn.silu(preact).astype(jnp.bfloat16)
    partial_out = jnp.dot(hidden, local_out, preferred_element_type=jnp.float32).astype(
        jnp.bfloat16
    )
    return partial_out.reshape(arriving.shape)


def expert_backward(row_part, grad_part, local_in, local_out):
    feature_width = row_part.shape[-1]
    preact = jnp.dot(
        row_part.reshape(-1, feature_width), local_in, preferred_element_type=jnp.float32
    )
    sigmoid_v = jax.nn.sigmoid(preact)
    slope_v = sigmoid_v * (1.0 + preact * (1.0 - sigmoid_v))
    grad_hidden = jnp.einsum(
        "rd,hd->rh",
        grad_part.reshape(-1, feature_width),
        local_out,
        preferred_element_type=jnp.float32,
    )
    grad_pre = (grad_hidden * slope_v).astype(jnp.bfloat16)
    partial_grad = jnp.einsum(
        "rh,dh->rd", grad_pre, local_in, preferred_element_type=jnp.float32
    ).astype(jnp.bfloat16)
    return partial_grad.reshape(row_part.shape)


def gather_groups(returned, groups):
    feature_width = returned.shape[-1]
    summed = jnp.sum(
        returned.reshape(groups, GROUP, CAP, feature_width).astype(jnp.float32), axis=1
    )
    return summed.reshape(groups * CAP, feature_width)


def per_device(
    handoff,
    saved_inputs,
    cotangent,
    ids_forward,
    gates_forward,
    ids_backward,
    gates_backward,
    weight_in,
    weight_out,
):
    highest = lax.Precision.HIGHEST
    groups = lax.axis_size("expert") // GROUP
    segment_index = lax.axis_index("segment")
    last_segment = lax.axis_size("segment") - 1
    arrived = shifted(handoff, "segment", 1)
    inputs = jnp.where(segment_index == 0, handoff, arrived)[0]
    returned = shifted(cotangent, "segment", -1)
    upstream = jnp.where(segment_index == last_segment, cotangent, returned)[0]
    local_in = weight_in[0]
    local_out = weight_out[0]
    select_f, weigh_f = slot_tables(ids_forward[0], gates_forward[0], groups)
    picked = jnp.dot(
        select_f.astype(jnp.bfloat16), inputs, preferred_element_type=jnp.float32
    ).astype(jnp.bfloat16)
    select_b, weigh_b = slot_tables(ids_backward[0], gates_backward[0], groups)
    rows_back = jnp.dot(
        select_b.astype(jnp.bfloat16), saved_inputs[0], preferred_element_type=jnp.float32
    ).astype(jnp.bfloat16)
    grads_out = jnp.dot(
        weigh_b, upstream.astype(jnp.float32), precision=highest, preferred_element_type=jnp.float32
    ).astype(jnp.bfloat16)
    backward_stack = jnp.stack([rows_back, grads_out])
    arriving_f = lax.all_to_all(
        pack_direct(picked[None], groups), "expert", split_axis=1, concat_axis=1, tiled=True
    )
    arriving_b = lax.all_to_all(
        pack_direct(backward_stack, groups), "expert", split_axis=1, concat_axis=1, tiled=True
    )
    partial_f = expert_forward(arriving_f[0], local_in, local_out)
    back_f = lax.all_to_all(partial_f, "expert", split_axis=0, concat_axis=0, tiled=True)
    combined = gather_groups(back_f, groups)
    expert_mix = jnp.dot(
        weigh_f.T, combined, precision=highest, preferred_element_type=jnp.float32
    ).astype(jnp.bfloat16)
    partial_b = expert_backward(arriving_b[0], arriving_b[1], local_in, local_out)
    back_b = lax.all_to_all(partial_b, "expert", split_axis=0, concat_axis=0, tiled=True)
    slot_grads = gather_groups(back_b, groups)
    input_grads = jnp.dot(
        select_b.T, slot_grads, precision=highest, preferred_element_type=jnp.float32
    ).astype(jnp.bfloat16)
    return (expert_mix[None], input_grads[None])


MESH = pl.DeviceIdType.MESH
BLOCK = 16
THIRDS = 3
PARTS = 2
LANES = 128


def flipped(position, mask):
    bit = 1
    while bit <= mask:
        if mask & bit:
            position = position + bit * (1 - 2 * ((position // bit) % 2))
        bit *= 2
    return position


def exchange_kernel(
    planes,
    chunk,
    ids_f_hbm,
    gates_f_hbm,
    ids_b_hbm,
    gates_b_hbm,
    handoff,
    saved,
    cotangent,
    weight_in,
    weight_out,
    sums,
    places,
    gate_wide,
    rows_x,
    rows_s,
    w_first,
    w_second,
    blocks,
    req_send,
    req_recv,
    late_send,
    slope,
    y_send,
    y_keep,
    y_recv,
    z_send,
    z_recv,
    own_sum,
    ids_f,
    gates_f,
    ids_b,
    gates_b,
    local_sem,
    send_sem,
    recv_sem,
):
    segment = lax.axis_index("segment")
    expert = lax.axis_index("expert")
    row_count, width = rows_x.shape
    hidden = weight_out.shape[0]
    tail = chunk // CAP
    rest = THIRDS * chunk

    def at_expert(mask):
        return {"expert": flipped(expert, mask)}

    def at_other(k):
        return {"segment": 1 - segment, "expert": flipped(expert, 4 * k)}

    sibling = at_expert(1)
    across = at_expert(2)
    mates = [None] + [at_expert(4 * k) for k in range(1, planes)]
    others = [at_other(k) for k in range(planes)]

    barrier = pltpu.get_barrier_semaphore()
    partners = mates[1:] + others + [across, sibling]
    for partner in partners:
        pl.semaphore_signal(barrier, inc=1, device_id=partner, device_id_type=MESH)

    tables = [
        pltpu.make_async_copy(source, target, local_sem.at[4 + i])
        for i, (source, target) in enumerate(
            [(ids_f_hbm, ids_f), (gates_f_hbm, gates_f), (ids_b_hbm, ids_b), (gates_b_hbm, gates_b)]
        )
    ]
    for table_copy in tables:
        table_copy.start()

    @pl.when(segment == 0)
    def _():
        pltpu.make_async_copy(handoff, rows_x, local_sem.at[0]).start()

    @pl.when(segment != 0)
    def _():
        pltpu.make_async_copy(cotangent, rows_x, local_sem.at[0]).start()

    load_x = pltpu.make_async_copy(handoff, rows_x, local_sem.at[0])
    load_s = pltpu.make_async_copy(saved, rows_s, local_sem.at[1])
    load_in = pltpu.make_async_copy(weight_in, w_first.at[0, :, 0:hidden], local_sem.at[2])
    load_out = pltpu.make_async_copy(weight_out, w_second.at[0, 0:hidden, :], local_sem.at[3])
    load_s.start()
    load_in.start()
    load_out.start()

    count = [0]

    def landing():
        count[0] += 1
        return recv_sem.at[count[0] - 1]

    def remote(source, target, device, leaving, arriving):
        return pltpu.make_async_remote_copy(
            src_ref=source,
            dst_ref=target,
            send_sem=leaving,
            recv_sem=arriving,
            device_id=device,
            device_id_type=MESH,
        )

    plane = expert // 4
    inner = (plane > 0) & (plane < planes - 1)

    def start_inner(copies):
        @pl.when(inner)
        def _():
            for copy in copies:
                copy.start()

    parts = range(PARTS)
    edges = [CAP * i // PARTS for i in range(PARTS + 1)]
    cuts = [slice(tail * low, tail * high) for low, high in zip(edges[:-1], edges[1:])]

    request = remote(req_send, req_recv, others[0], send_sem.at[0], landing())
    give_in = remote(weight_in, w_first.at[0, :, hidden : 2 * hidden], sibling, send_sem.at[1], landing())
    give_out = remote(weight_out, w_second.at[0, hidden : 2 * hidden, :], sibling, send_sem.at[2], landing())

    def ship(source, target, device, leaving, arriving):
        return [
            remote(source.at[:, cut], target.at[:, cut], device, leaving, arriving[part])
            for part, cut in enumerate(cuts)
        ]

    def block(kind, k, side=0):
        return blocks.at[(kind * planes + k) * 2 + side]

    far = planes - 1
    gathers, inners, reduces = send_sem.at[3], send_sem.at[4], send_sem.at[5]
    land_z = [[[landing() for part in parts] for k in range(planes)] for kind in range(3)]
    land_y = [[landing()] * PARTS for kind in range(3)]
    land_back_y = [[[landing() for part in parts] for k in range(planes)] for o in range(2)]
    land_back_z = [[landing()] * PARTS for o in range(2)]
    gather_z = []
    for kind in range(3):
        sources = [late_send if kind == 2 else block(kind, 0)] * planes
        targets = others if kind == 2 else mates
        gather_z.append(
            [
                None
                if targets[k] is None
                else ship(sources[k], block(kind, k), targets[k], inners if k == far else gathers, land_z[kind][k])
                for k in range(planes)
            ]
        )
    forward_z = [ship(block(kind, 2), block(kind, far), mates[1], inners, land_z[kind][far]) for kind in range(3)]
    gather_y = [
        [ship(block(kind, k), block(kind, k, 1), across, gathers, land_y[kind]) for k in range(planes)]
        for kind in range(3)
    ]
    reduce_y = [
        [ship(y_send.at[o, k], y_recv.at[o, k], across, reduces, land_back_y[o][k]) for k in range(planes)]
        for o in range(2)
    ]
    reduce_z = [
        [None] + [ship(z_send.at[o, k], z_recv.at[o, k], mates[k], reduces, land_back_z[o]) for k in range(1, planes)]
        for o in range(2)
    ]

    def whole(number, leaving, arriving):
        return remote(blocks.at[0:number], blocks.at[0:number], across, leaving, arriving)

    for table_copy in tables:
        table_copy.wait()
    earlier = jnp.where(
        lax.broadcasted_iota(jnp.int32, (row_count, row_count), 0)
        < lax.broadcasted_iota(jnp.int32, (row_count, row_count), 1),
        1.0,
        0.0,
    ).astype(jnp.bfloat16)
    block_row = lax.broadcasted_iota(jnp.int32, (BLOCK, row_count), 0)
    third = sum((block_row >= CAP * q).astype(jnp.int32) for q in range(1, THIRDS + 1))
    slot = block_row - CAP * third

    def ranks(ids, gates):
        first, second = ids[0:1, :] == 0, ids[1:2, :] == 0
        member = jnp.where(first | second, 1.0, 0.0)
        gate = jnp.where(first, gates[0:1, :], 0.0) + jnp.where(second, gates[1:2, :], 0.0)
        wide = jnp.broadcast_to(member, (BLOCK, row_count))
        rank = jnp.dot(wide.astype(jnp.bfloat16), earlier, preferred_element_type=jnp.float32)
        placed = jnp.where((slot == rank.astype(jnp.int32)) & (third < THIRDS), wide, 0.0)
        return placed, gate

    placed_f, gate_f = ranks(ids_f, gates_f)
    placed_b, gate_b = ranks(ids_b, gates_b)
    later = (segment * jnp.ones((), jnp.int32)).astype(jnp.float32)
    scaled_b = placed_b * gate_b
    asked = scaled_b * (1.0 - later) + placed_f * later
    mine = placed_f * (1.0 - later) + scaled_b * later
    req_send[...] = jnp.concatenate([asked, jnp.zeros((BLOCK, LANES - row_count), jnp.float32)], axis=1)
    pl.semaphore_wait(barrier, len(partners))
    request.start()

    def pick(weights, rows_ref, target):
        ending = jnp.concatenate(
            [jnp.where(block_row == BLOCK - 1, weights[i : i + 1, :], 0.0) for i in range(CAP)], axis=0
        )

        def product(chosen, columns):
            return jnp.dot(
                jnp.where(chosen, 1.0, 0.0).astype(jnp.bfloat16),
                rows_ref[:, columns],
                preferred_element_type=jnp.float32,
            )

        scale = jnp.sum(weights, axis=1, keepdims=True)
        chosen = [(weights != 0.0) & (third == q) for q in range(THIRDS)]
        last = product(ending != 0.0, slice(rest, width)) * jnp.sum(ending, axis=1, keepdims=True)
        for i in range(CAP):
            total = sum(
                product(chosen[q], slice(q * chunk + i * tail, q * chunk + (i + 1) * tail)) for q in range(THIRDS)
            )
            value = total * scale + last[i * BLOCK : (i + 1) * BLOCK]
            target[:, i * tail : (i + 1) * tail] = value.astype(jnp.bfloat16)

    def spread(kind):
        for part in parts:
            gather_y[kind][0][part].start()
            for k in range(1, far):
                gather_z[kind][k][part].start()
        start_inner(gather_z[kind][far])

    load_x.wait()
    pick(mine, rows_x, block(0, 0))
    spread(0)
    load_s.wait()
    pick(placed_b, rows_s, block(1, 0))
    spread(1)
    give_in.start()
    give_out.start()
    request.wait_recv()
    pick(req_recv[:, 0:row_count], rows_x, late_send)
    for part in parts:
        for k in range(far):
            gather_z[2][k][part].start()
    start_inner(gather_z[2][far])

    turn = 512 if width % 512 == 0 else LANES

    def transpose(low, share=0, shares=1):
        half = slice(low, low + hidden)

        def step(number, carry):
            piece = pl.ds(pl.multiple_of(number * turn, turn), turn)
            w_first[1, piece, half] = w_second[0, half, piece].T
            w_second[1, half, piece] = w_first[0, piece, half].T
            return carry

        steps = width // turn
        lax.fori_loop(steps * share // shares, steps * (share + 1) // shares, step, 0)

    def relay(kind, k):
        for part in parts:
            gather_z[kind][k][part].wait_recv()
            if k == 2:
                start_inner([forward_z[kind][part]])
            gather_y[kind][k][part].start()

    def relays(outer_order, inner_order):
        @pl.when(inner)
        def _():
            for kind, k in inner_order:
                relay(kind, k)

        @pl.when(jnp.logical_not(inner))
        def _():
            for kind, k in outer_order:
                relay(kind, k)

    load_in.wait()
    load_out.wait()
    transpose(0)
    relays([(0, 1), (0, 2), (1, 1)], [(0, 1), (0, 3), (0, 2), (1, 1)])
    relays([(2, 0)], [(1, 3), (2, 0)])
    give_in.wait_recv()
    give_out.wait_recv()
    transpose(hidden, 0, 2)
    relays([(1, 2), (2, 1)], [(1, 2), (2, 1)])
    transpose(hidden, 1, 2)
    relays([(0, 3), (2, 2), (1, 3)], [(2, 3), (2, 2)])
    unit = jnp.where(
        lax.broadcasted_iota(jnp.int32, (row_count, row_count), 0)
        == lax.broadcasted_iota(jnp.int32, (row_count, row_count), 1),
        1.0,
        0.0,
    )
    by_row = (((1,), (1,)), ((), ()))
    for i, placed in enumerate([placed_f, placed_b]):
        places[i] = lax.dot_general(
            unit.astype(jnp.bfloat16),
            placed.astype(jnp.bfloat16),
            by_row,
            preferred_element_type=jnp.float32,
        ).astype(jnp.bfloat16)
    gate_wide[...] = lax.dot_general(
        unit,
        jnp.broadcast_to(gate_f, (LANES, row_count)),
        by_row,
        precision=lax.Precision.HIGHEST,
        preferred_element_type=jnp.float32,
    )

    batch = 2 * planes * BLOCK
    place = lax.broadcasted_iota(jnp.int32, (batch, 2 * hidden), 0) % BLOCK

    def arrived(kind):
        whole(planes, gathers, land_y[kind][0]).wait_recv()

    def contract(kind, side):
        gathered = blocks[2 * planes * kind : 2 * planes * (kind + 1)].reshape(batch, chunk)

        def product(columns, rows):
            return jnp.dot(gathered[:, columns], w_first[side, rows, :], preferred_element_type=jnp.float32)

        value = product(slice(0, chunk), slice(0, chunk))
        for q in range(1, THIRDS):
            value = value + pltpu.roll(
                product(slice(0, chunk), slice(q * chunk, (q + 1) * chunk)), batch - CAP * q, 0
            )
        for i in range(CAP):
            last = product(slice(i * tail, (i + 1) * tail), slice(rest, width))
            value = value + jnp.where(place == i, pltpu.roll(last, batch - (BLOCK - 1 - i), 0), 0.0)
        return value

    def sigmoid(value):
        return 1.0 / (1.0 + jnp.exp(-value))

    order = [k for k in range(planes - 1, -1, -1)]

    def expand(value, side, o):
        value = jnp.where(place < CAP, value, 0.0)
        left = [value.astype(jnp.bfloat16)]
        left += [pltpu.roll(value, CAP * q, 0).astype(jnp.bfloat16) for q in range(1, THIRDS)]
        for part in parts:
            for i in range(edges[part], edges[part + 1]):
                piece = slice(i * tail, (i + 1) * tail)
                total = sum(
                    jnp.dot(
                        left[q],
                        w_second[side, :, q * chunk + i * tail : q * chunk + (i + 1) * tail],
                        preferred_element_type=jnp.float32,
                    )
                    for q in range(THIRDS)
                )
                last = jnp.where(place == BLOCK - 1, pltpu.roll(value, BLOCK - 1 - i, 0), 0.0)
                total = total + jnp.dot(
                    last.astype(jnp.bfloat16), w_second[side, :, rest:width], preferred_element_type=jnp.float32
                )
                total = total.reshape(planes, 2, BLOCK, tail)
                y_keep[o, :, :, piece] = total[:, 0]
                y_send[o, :, :, piece] = total[:, 1].astype(jnp.bfloat16)
            for k in order:
                reduce_y[o][k][part].start()

    def join(o, part):
        cut = cuts[part]
        for k in order:
            reduce_y[o][k][part].wait_recv()
            total = y_keep[o, k, :, cut] + y_recv[o, k, :, cut].astype(jnp.float32)
            if k == 0:
                own_sum[o, :, cut] = total
            else:
                z_send[o, k, :, cut] = total.astype(jnp.bfloat16)
                reduce_z[o][k][part].start()

    arrived(0)
    first = contract(0, segment)
    relays([(2, 3)], [])
    arrived(1)
    pre = contract(1, 0)
    gate = sigmoid(pre)
    slope[...] = gate * (1.0 + pre * (1.0 - gate))
    expand(first * sigmoid(first) * (1.0 - later) + first * slope[...] * later, segment, 0)
    arrived(2)
    last = contract(2, 1 - segment)
    expand(last * slope[...] * (1.0 - later) + last * sigmoid(last) * later, 1 - segment, 1)
    for o in range(2):
        for part in parts:
            join(o, part)
    for o in range(2):
        whole(planes - 1, reduces, land_back_z[o][0]).wait_recv()
        total = own_sum[o]
        for k in range(1, planes):
            total = total + z_recv[o, k].astype(jnp.float32)
        sums[segment if o == 0 else 1 - segment] = total.astype(jnp.bfloat16)
    request.wait_send()
    give_in.wait_send()
    give_out.wait_send()
    whole(5 * planes - 1, gathers, land_y[0][0]).wait_send()
    whole(4 * planes - 2, reduces, land_y[0][0]).wait_send()

    @pl.when(inner)
    def _():
        whole(6, inners, land_y[0][0]).wait_send()


def scatter_kernel(chunk, sums, places, gate_wide, out_f, out_b):
    width = out_f.shape[1]
    column = lax.broadcasted_iota(jnp.int32, places.shape[1:], 1)
    gate = gate_wide[:, 0:1]
    tail = chunk // CAP

    def product(i, chosen, columns):
        return jnp.dot(chosen.astype(jnp.bfloat16), sums[i, :, columns], preferred_element_type=jnp.float32)

    for i, out in enumerate([out_f, out_b]):
        placed = places[i].astype(jnp.float32)

        def put(columns, value):
            out[:, columns] = (value * gate if i == 0 else value).astype(jnp.bfloat16)

        for q in range(THIRDS):
            inside = (column >= CAP * q) & (column < CAP * (q + 1))
            put(slice(q * chunk, (q + 1) * chunk), product(i, jnp.where(inside, placed, 0.0), slice(0, chunk)))
        put(
            slice(THIRDS * chunk, width),
            sum(
                product(
                    i,
                    jnp.where(column == BLOCK - 1, placed[:, slot : slot + 1], 0.0),
                    slice(slot * tail, (slot + 1) * tail),
                )
                for slot in range(CAP)
            ),
        )


def exchange(planes, handoff, saved_inputs, cotangent, ids_forward, gates_forward, ids_backward, gates_backward, weight_in, weight_out):
    rows, width = handoff.shape[1:]
    hidden = weight_out.shape[1]
    chunk = width // BLOCK * CAP
    bf16, f32 = jnp.bfloat16, jnp.float32
    landings = 3 + PARTS * 5 * planes + 5
    vmem = pl.BlockSpec(memory_space=pltpu.VMEM)
    hbm = pl.BlockSpec(memory_space=pl.ANY)
    sums, places, gate_wide = pl.pallas_call(
        functools.partial(exchange_kernel, planes, chunk),
        out_shape=[
            pltpu.VMEM((2, BLOCK, chunk), bf16),
            pltpu.VMEM((2, rows, BLOCK), bf16),
            pltpu.VMEM((rows, LANES), f32),
        ],
        in_specs=[hbm] * 9,
        out_specs=[vmem] * 3,
        scratch_shapes=[
            pltpu.VMEM((rows, width), bf16),
            pltpu.VMEM((rows, width), bf16),
            pltpu.VMEM((2, width, 2 * hidden), bf16),
            pltpu.VMEM((2, 2 * hidden, width), bf16),
            pltpu.VMEM((6 * planes, BLOCK, chunk), bf16),
            pltpu.VMEM((BLOCK, LANES), f32),
            pltpu.VMEM((BLOCK, LANES), f32),
            pltpu.VMEM((BLOCK, chunk), bf16),
            pltpu.VMEM((2 * planes * BLOCK, 2 * hidden), f32),
            pltpu.VMEM((2, planes, BLOCK, chunk), bf16),
            pltpu.VMEM((2, planes, BLOCK, chunk), f32),
            pltpu.VMEM((2, planes, BLOCK, chunk), bf16),
            pltpu.VMEM((2, planes, BLOCK, chunk), bf16),
            pltpu.VMEM((2, planes, BLOCK, chunk), bf16),
            pltpu.VMEM((2, BLOCK, chunk), f32),
            pltpu.VMEM((2, rows), jnp.int32),
            pltpu.VMEM((2, rows), f32),
            pltpu.VMEM((2, rows), jnp.int32),
            pltpu.VMEM((2, rows), f32),
            pltpu.SemaphoreType.DMA((8,)),
            pltpu.SemaphoreType.DMA((6,)),
            pltpu.SemaphoreType.DMA((landings,)),
        ],
        compiler_params=pltpu.CompilerParams(
            collective_id=0, has_side_effects=True
        ),
    )(
        ids_forward[0].T,
        gates_forward[0].T,
        ids_backward[0].T,
        gates_backward[0].T,
        handoff[0],
        saved_inputs[0],
        cotangent[0],
        weight_in[0],
        weight_out[0],
    )
    mixed, grads = pl.pallas_call(
        functools.partial(scatter_kernel, chunk),
        out_shape=[jax.ShapeDtypeStruct((rows, width), bf16)] * 2,
        in_specs=[vmem] * 3,
        out_specs=[vmem] * 2,
    )(*[pltpu.with_memory_space_constraint(x, pltpu.VMEM) for x in (sums, places, gate_wide)])
    return (mixed[None], grads[None])


def device_body(mesh):
    segments, experts = mesh.shape["segment"], mesh.shape["expert"]
    planes = experts // 4
    if segments == 2 and experts == GROUP and planes == 4:
        return functools.partial(exchange, planes)
    return per_device


def solution(mesh):
    return jax.shard_map(
        device_body(mesh),
        mesh=mesh,
        in_specs=(
            P("segment", "expert", None),
            P("segment", "expert", None),
            P("segment", "expert", None),
            P("segment", "expert", None),
            P("segment", "expert", None),
            P("segment", "expert", None),
            P("segment", "expert", None),
            P("segment", None, "expert"),
            P("segment", "expert", None),
        ),
        out_specs=(P("segment", "expert", None), P("segment", "expert", None)),
        check_vma=False,
    )
```

```python
import functools

import jax
import jax.numpy as jnp
from jax import lax
from jax.experimental import pallas as pl
from jax.experimental.pallas import tpu as pltpu
from jax.sharding import PartitionSpec as P

GROUP = 16
CAP = 5


def shifted(block, axis, distance):
    devices = range(lax.axis_size(axis))
    route = [(i - distance, i) for i in devices if i - distance in devices]
    return lax.ppermute(block, axis, route)


def slot_tables(expert_ids, gate_values, experts):
    row_count = expert_ids.shape[0]
    flat_ids = expert_ids.reshape(row_count * 2)
    window = jnp.arange(experts, dtype=jnp.int32)
    member = (flat_ids[None, :] == window[:, None]).astype(jnp.int32)
    before = jnp.cumsum(member, axis=1, dtype=jnp.int32) - member
    positions = jnp.arange(CAP, dtype=jnp.int32)
    picked_slots = (
        member[:, None, :] * (before[:, None, :] == positions[None, :, None]).astype(jnp.int32)
    ).astype(jnp.float32)
    picked_slots = picked_slots.reshape(experts * CAP, row_count, 2)
    select = jnp.sum(picked_slots, axis=2)
    weighted = jnp.sum(picked_slots * gate_values[None, :, :], axis=2)
    return (select, weighted)


def pack_direct(stacked, groups):
    stacks = stacked.shape[0]
    feature_width = stacked.shape[2]
    shaped = stacked.reshape(stacks, groups, 1, CAP, feature_width)
    spread_out = jnp.broadcast_to(shaped, (stacks, groups, GROUP, CAP, feature_width))
    return spread_out.reshape(stacks, groups * GROUP, CAP, feature_width)


def expert_forward(arriving, local_in, local_out):
    feature_width = arriving.shape[-1]
    preact = jnp.dot(
        arriving.reshape(-1, feature_width), local_in, preferred_element_type=jnp.float32
    )
    hidden = jax.nn.silu(preact).astype(jnp.bfloat16)
    partial_out = jnp.dot(hidden, local_out, preferred_element_type=jnp.float32).astype(
        jnp.bfloat16
    )
    return partial_out.reshape(arriving.shape)


def expert_backward(row_part, grad_part, local_in, local_out):
    feature_width = row_part.shape[-1]
    preact = jnp.dot(
        row_part.reshape(-1, feature_width), local_in, preferred_element_type=jnp.float32
    )
    sigmoid_v = jax.nn.sigmoid(preact)
    slope_v = sigmoid_v * (1.0 + preact * (1.0 - sigmoid_v))
    grad_hidden = jnp.einsum(
        "rd,hd->rh",
        grad_part.reshape(-1, feature_width),
        local_out,
        preferred_element_type=jnp.float32,
    )
    grad_pre = (grad_hidden * slope_v).astype(jnp.bfloat16)
    partial_grad = jnp.einsum(
        "rh,dh->rd", grad_pre, local_in, preferred_element_type=jnp.float32
    ).astype(jnp.bfloat16)
    return partial_grad.reshape(row_part.shape)


def gather_groups(returned, groups):
    feature_width = returned.shape[-1]
    summed = jnp.sum(
        returned.reshape(groups, GROUP, CAP, feature_width).astype(jnp.float32), axis=1
    )
    return summed.reshape(groups * CAP, feature_width)


def per_device(
    handoff,
    saved_inputs,
    cotangent,
    ids_forward,
    gates_forward,
    ids_backward,
    gates_backward,
    weight_in,
    weight_out,
):
    highest = lax.Precision.HIGHEST
    groups = lax.axis_size("expert") // GROUP
    segment_index = lax.axis_index("segment")
    last_segment = lax.axis_size("segment") - 1
    arrived = shifted(handoff, "segment", 1)
    inputs = jnp.where(segment_index == 0, handoff, arrived)[0]
    returned = shifted(cotangent, "segment", -1)
    upstream = jnp.where(segment_index == last_segment, cotangent, returned)[0]
    local_in = weight_in[0]
    local_out = weight_out[0]
    select_f, weigh_f = slot_tables(ids_forward[0], gates_forward[0], groups)
    picked = jnp.dot(
        select_f.astype(jnp.bfloat16), inputs, preferred_element_type=jnp.float32
    ).astype(jnp.bfloat16)
    select_b, weigh_b = slot_tables(ids_backward[0], gates_backward[0], groups)
    rows_back = jnp.dot(
        select_b.astype(jnp.bfloat16), saved_inputs[0], preferred_element_type=jnp.float32
    ).astype(jnp.bfloat16)
    grads_out = jnp.dot(
        weigh_b, upstream.astype(jnp.float32), precision=highest, preferred_element_type=jnp.float32
    ).astype(jnp.bfloat16)
    backward_stack = jnp.stack([rows_back, grads_out])
    arriving_f = lax.all_to_all(
        pack_direct(picked[None], groups), "expert", split_axis=1, concat_axis=1, tiled=True
    )
    arriving_b = lax.all_to_all(
        pack_direct(backward_stack, groups), "expert", split_axis=1, concat_axis=1, tiled=True
    )
    partial_f = expert_forward(arriving_f[0], local_in, local_out)
    back_f = lax.all_to_all(partial_f, "expert", split_axis=0, concat_axis=0, tiled=True)
    combined = gather_groups(back_f, groups)
    expert_mix = jnp.dot(
        weigh_f.T, combined, precision=highest, preferred_element_type=jnp.float32
    ).astype(jnp.bfloat16)
    partial_b = expert_backward(arriving_b[0], arriving_b[1], local_in, local_out)
    back_b = lax.all_to_all(partial_b, "expert", split_axis=0, concat_axis=0, tiled=True)
    slot_grads = gather_groups(back_b, groups)
    input_grads = jnp.dot(
        select_b.T, slot_grads, precision=highest, preferred_element_type=jnp.float32
    ).astype(jnp.bfloat16)
    return (expert_mix[None], input_grads[None])


MESH = pl.DeviceIdType.MESH
BLOCK = 16
THIRDS = 3
PARTS = 2
LANES = 128
GATHER_CROSS = (0,)
REDUCE_CROSS = (0, 1)


def flipped(position, mask):
    bit = 1
    while bit <= mask:
        if mask & bit:
            position = position + bit * (1 - 2 * ((position // bit) % 2))
        bit *= 2
    return position


def exchange_kernel(
    planes,
    chunk,
    ids_f_hbm,
    gates_f_hbm,
    ids_b_hbm,
    gates_b_hbm,
    handoff,
    saved,
    cotangent,
    weight_in,
    weight_out,
    sums,
    places,
    gate_wide,
    rows_x,
    rows_s,
    w_first,
    w_second,
    blocks,
    req_send,
    req_recv,
    late_send,
    slope,
    y_send,
    y_keep,
    y_recv,
    cross_keep,
    cross_recv,
    z_send,
    z_recv,
    own_sum,
    ids_f,
    gates_f,
    ids_b,
    gates_b,
    local_sem,
    send_sem,
    recv_sem,
):
    segment = lax.axis_index("segment")
    expert = lax.axis_index("expert")
    row_count, width = rows_x.shape
    hidden = weight_out.shape[0]
    tail = chunk // CAP
    rest = THIRDS * chunk

    def at_expert(mask):
        return {"expert": flipped(expert, mask)}

    def at_other(k):
        return {"segment": 1 - segment, "expert": flipped(expert, 4 * k)}

    sibling = at_expert(1)
    across = at_expert(2)
    mates = [None] + [at_expert(4 * k) for k in range(1, planes)]
    others = [at_other(k) for k in range(planes)]

    barrier = pltpu.get_barrier_semaphore()
    plane = expert // 4
    inner = (plane > 0) & (plane < planes - 1)
    partners = [across, sibling, others[0]] + mates[1 : planes - 1]
    for partner in partners:
        pl.semaphore_signal(barrier, inc=1, device_id=partner, device_id_type=MESH)

    @pl.when(inner)
    def _():
        pl.semaphore_signal(barrier, inc=1, device_id=mates[-1], device_id_type=MESH)


    tables = [
        pltpu.make_async_copy(source, target, local_sem.at[4 + i])
        for i, (source, target) in enumerate(
            [(ids_f_hbm, ids_f), (gates_f_hbm, gates_f), (ids_b_hbm, ids_b), (gates_b_hbm, gates_b)]
        )
    ]
    for table_copy in tables:
        table_copy.start()

    @pl.when(segment == 0)
    def _():
        pltpu.make_async_copy(handoff, rows_x, local_sem.at[0]).start()

    @pl.when(segment != 0)
    def _():
        pltpu.make_async_copy(cotangent, rows_x, local_sem.at[0]).start()

    load_x = pltpu.make_async_copy(handoff, rows_x, local_sem.at[0])
    load_s = pltpu.make_async_copy(saved, rows_s, local_sem.at[1])
    load_in = pltpu.make_async_copy(weight_in, w_first.at[0, :, 0:hidden], local_sem.at[2])
    load_out = pltpu.make_async_copy(weight_out, w_second.at[0, 0:hidden, :], local_sem.at[3])
    load_s.start()
    load_in.start()
    load_out.start()

    count = [0]

    def landing():
        count[0] += 1
        return recv_sem.at[count[0] - 1]

    def remote(source, target, device, leaving, arriving):
        return pltpu.make_async_remote_copy(
            src_ref=source,
            dst_ref=target,
            send_sem=leaving,
            recv_sem=arriving,
            device_id=device,
            device_id_type=MESH,
        )

    def start_inner(copies):
        @pl.when(inner)
        def _():
            for copy in copies:
                copy.start()

    parts = range(PARTS)
    edges = [CAP * i // PARTS for i in range(PARTS + 1)]
    cuts = [slice(tail * low, tail * high) for low, high in zip(edges[:-1], edges[1:])]

    request = remote(req_send, req_recv, others[0], send_sem.at[0], landing())
    give_in = remote(weight_in, w_first.at[0, :, hidden : 2 * hidden], sibling, send_sem.at[1], landing())
    give_out = remote(weight_out, w_second.at[0, hidden : 2 * hidden, :], sibling, send_sem.at[2], landing())

    def ship(source, target, device, leaving, arriving):
        return [
            remote(source.at[:, cut], target.at[:, cut], device, leaving, arriving[part])
            for part, cut in enumerate(cuts)
        ]

    def block(kind, k, side=0):
        return blocks.at[(kind * planes + k) * 2 + side]

    far = planes - 1
    gathers, inners, reduces = send_sem.at[3], send_sem.at[4], send_sem.at[5]
    land_z = [[[landing() for part in parts] for k in range(planes)] for kind in range(3)]
    land_y = [[landing()] * PARTS for kind in range(3)]
    land_near = [[landing() for part in parts] for kind in range(3)]
    land_cross = [[landing() for part in parts] for o in range(2)]
    land_back_y = [[[landing() for part in parts] for k in range(planes)] for o in range(2)]
    land_back_z = [[landing()] * PARTS for o in range(2)]
    gather_z = []
    for kind in range(3):
        sources = [late_send if kind == 2 else block(kind, 0)] * planes
        targets = others if kind == 2 else mates
        gather_z.append(
            [
                None
                if targets[k] is None
                else ship(sources[k], block(kind, k), targets[k], inners if k == far else gathers, land_z[kind][k])
                for k in range(planes)
            ]
        )
    forward_z = [ship(block(kind, 2), block(kind, far), mates[1], inners, land_z[kind][far]) for kind in range(3)]
    gather_y = [
        [
            ship(block(kind, k), block(kind, k, 1), across, gathers, land_y[kind] if k else land_near[kind])
            for k in range(planes)
        ]
        for kind in range(3)
    ]
    gather_cross = [
        ship(block(kind, 0, 1), block(kind, 1, 1), mates[1], gathers, land_y[kind]) for kind in range(3)
    ]
    reduce_cross = [ship(y_send.at[o, 1], cross_recv.at[o], mates[1], reduces, land_cross[o]) for o in range(2)]
    reduce_y = [
        [ship(y_send.at[o, k], y_recv.at[o, k], across, reduces, land_back_y[o][k]) for k in range(planes)]
        for o in range(2)
    ]
    reduce_z = [
        [None] + [ship(z_send.at[o, k], z_recv.at[o, k], mates[k], reduces, land_back_z[o]) for k in range(1, planes)]
        for o in range(2)
    ]

    def whole(number, leaving, arriving):
        return remote(blocks.at[0:number], blocks.at[0:number], across, leaving, arriving)

    for table_copy in tables:
        table_copy.wait()
    earlier = jnp.where(
        lax.broadcasted_iota(jnp.int32, (row_count, row_count), 0)
        < lax.broadcasted_iota(jnp.int32, (row_count, row_count), 1),
        1.0,
        0.0,
    ).astype(jnp.bfloat16)
    block_row = lax.broadcasted_iota(jnp.int32, (BLOCK, row_count), 0)
    third = sum((block_row >= CAP * q).astype(jnp.int32) for q in range(1, THIRDS + 1))
    slot = block_row - CAP * third

    def ranks(ids, gates):
        first, second = ids[0:1, :] == 0, ids[1:2, :] == 0
        member = jnp.where(first | second, 1.0, 0.0)
        gate = jnp.where(first, gates[0:1, :], 0.0) + jnp.where(second, gates[1:2, :], 0.0)
        wide = jnp.broadcast_to(member, (BLOCK, row_count))
        rank = jnp.dot(wide.astype(jnp.bfloat16), earlier, preferred_element_type=jnp.float32)
        placed = jnp.where((slot == rank.astype(jnp.int32)) & (third < THIRDS), wide, 0.0)
        return placed, gate

    placed_f, gate_f = ranks(ids_f, gates_f)
    placed_b, gate_b = ranks(ids_b, gates_b)
    later = (segment * jnp.ones((), jnp.int32)).astype(jnp.float32)
    scaled_b = placed_b * gate_b
    asked = scaled_b * (1.0 - later) + placed_f * later
    mine = placed_f * (1.0 - later) + scaled_b * later
    req_send[...] = jnp.concatenate([asked, jnp.zeros((BLOCK, LANES - row_count), jnp.float32)], axis=1)

    @pl.when(inner)
    def _():
        pl.semaphore_wait(barrier, len(partners) + 1)

    @pl.when(jnp.logical_not(inner))
    def _():
        pl.semaphore_wait(barrier, len(partners))

    request.start()

    def pick(weights, rows_ref, target):
        ending = jnp.concatenate(
            [jnp.where(block_row == BLOCK - 1, weights[i : i + 1, :], 0.0) for i in range(CAP)], axis=0
        )

        def product(chosen, columns):
            return jnp.dot(
                jnp.where(chosen, 1.0, 0.0).astype(jnp.bfloat16),
                rows_ref[:, columns],
                preferred_element_type=jnp.float32,
            )

        scale = jnp.sum(weights, axis=1, keepdims=True)
        chosen = [(weights != 0.0) & (third == q) for q in range(THIRDS)]
        last = product(ending != 0.0, slice(rest, width)) * jnp.sum(ending, axis=1, keepdims=True)
        for i in range(CAP):
            total = sum(
                product(chosen[q], slice(q * chunk + i * tail, q * chunk + (i + 1) * tail)) for q in range(THIRDS)
            )
            value = total * scale + last[i * BLOCK : (i + 1) * BLOCK]
            target[:, i * tail : (i + 1) * tail] = value.astype(jnp.bfloat16)

    def spread(kind):
        for part in parts:
            gather_y[kind][0][part].start()
            for k in range(1, far):
                gather_z[kind][k][part].start()
        start_inner(gather_z[kind][far])

    load_x.wait()
    pick(mine, rows_x, block(0, 0))
    spread(0)
    load_s.wait()
    pick(placed_b, rows_s, block(1, 0))
    spread(1)
    give_in.start()
    give_out.start()
    turn = 512 if width % 512 == 0 else LANES

    def transpose(low, share=0, shares=1):
        half = slice(low, low + hidden)

        def step(number, carry):
            piece = pl.ds(pl.multiple_of(number * turn, turn), turn)
            w_first[1, piece, half] = w_second[0, half, piece].T
            w_second[1, half, piece] = w_first[0, piece, half].T
            return carry

        steps = width // turn
        lax.fori_loop(steps * share // shares, steps * (share + 1) // shares, step, 0)

    load_in.wait()
    load_out.wait()
    transpose(0)
    request.wait_recv()
    pick(req_recv[:, 0:row_count], rows_x, late_send)
    for part in parts:
        for k in range(far):
            gather_z[2][k][part].start()
    start_inner(gather_z[2][far])

    def relay(kind, k):
        for part in parts:
            gather_z[kind][k][part].wait_recv()
            if k == 2:
                start_inner([forward_z[kind][part]])
            if k != 1 or part not in GATHER_CROSS:
                gather_y[kind][k][part].start()

    def cross(kind):
        for part in parts:
            gather_y[kind][0][part].wait_recv()
            if part in GATHER_CROSS:
                gather_cross[kind][part].start()

    def relays(outer_order, inner_order):
        @pl.when(inner)
        def _():
            for kind, k in inner_order:
                relay(kind, k)

        @pl.when(jnp.logical_not(inner))
        def _():
            for kind, k in outer_order:
                relay(kind, k)

    relays([(0, 1), (0, 2), (1, 1)], [(0, 1), (0, 2), (0, 3), (1, 1)])
    cross(0)
    cross(1)
    relays([(2, 0)], [(1, 2), (1, 3)])
    give_in.wait_recv()
    give_out.wait_recv()
    transpose(hidden, 0, 2)
    relays([(1, 2), (2, 1)], [(2, 0), (2, 1)])
    transpose(hidden, 1, 2)
    relays([(0, 3), (2, 2), (1, 3)], [(2, 2), (2, 3)])
    cross(2)
    unit = jnp.where(
        lax.broadcasted_iota(jnp.int32, (row_count, row_count), 0)
        == lax.broadcasted_iota(jnp.int32, (row_count, row_count), 1),
        1.0,
        0.0,
    )
    by_row = (((1,), (1,)), ((), ()))
    for i, placed in enumerate([placed_f, placed_b]):
        places[i] = lax.dot_general(
            unit.astype(jnp.bfloat16),
            placed.astype(jnp.bfloat16),
            by_row,
            preferred_element_type=jnp.float32,
        ).astype(jnp.bfloat16)
    gate_wide[...] = lax.dot_general(
        unit,
        jnp.broadcast_to(gate_f, (LANES, row_count)),
        by_row,
        precision=lax.Precision.HIGHEST,
        preferred_element_type=jnp.float32,
    )

    batch = 2 * planes * BLOCK
    place = lax.broadcasted_iota(jnp.int32, (batch, 2 * hidden), 0) % BLOCK

    def arrived(kind):
        whole(planes - 1, gathers, land_y[kind][0]).wait_recv()

    def contract(kind, side):
        gathered = blocks[2 * planes * kind : 2 * planes * (kind + 1)].reshape(batch, chunk)

        def product(columns, rows):
            return jnp.dot(gathered[:, columns], w_first[side, rows, :], preferred_element_type=jnp.float32)

        value = product(slice(0, chunk), slice(0, chunk))
        for q in range(1, THIRDS):
            value = value + pltpu.roll(
                product(slice(0, chunk), slice(q * chunk, (q + 1) * chunk)), batch - CAP * q, 0
            )
        for i in range(CAP):
            last = product(slice(i * tail, (i + 1) * tail), slice(rest, width))
            value = value + jnp.where(place == i, pltpu.roll(last, batch - (BLOCK - 1 - i), 0), 0.0)
        return value

    def sigmoid(value):
        return 1.0 / (1.0 + jnp.exp(-value))

    order = [k for k in range(planes - 1, -1, -1)]

    def expand(value, side, o):
        value = jnp.where(place < CAP, value, 0.0)
        left = [value.astype(jnp.bfloat16)]
        left += [pltpu.roll(value, CAP * q, 0).astype(jnp.bfloat16) for q in range(1, THIRDS)]
        for part in parts:
            for i in range(edges[part], edges[part + 1]):
                piece = slice(i * tail, (i + 1) * tail)
                total = sum(
                    jnp.dot(
                        left[q],
                        w_second[side, :, q * chunk + i * tail : q * chunk + (i + 1) * tail],
                        preferred_element_type=jnp.float32,
                    )
                    for q in range(THIRDS)
                )
                last = jnp.where(place == BLOCK - 1, pltpu.roll(value, BLOCK - 1 - i, 0), 0.0)
                total = total + jnp.dot(
                    last.astype(jnp.bfloat16), w_second[side, :, rest:width], preferred_element_type=jnp.float32
                )
                total = total.reshape(planes, 2, BLOCK, tail)
                y_keep[o, :, :, piece] = total[:, 0]
                y_send[o, 1:planes, :, piece] = total[1:planes, 1].astype(jnp.bfloat16)
                if part in REDUCE_CROSS:
                    cross_keep[o, :, piece] = total[0, 1]
                    z_send[o, 1, :, piece] = total[1, 0].astype(jnp.bfloat16)
                else:
                    y_send[o, 0, :, piece] = total[0, 1].astype(jnp.bfloat16)
            if part in REDUCE_CROSS:
                reduce_cross[o][part].start()
            for k in order:
                if k > 1 or part not in REDUCE_CROSS:
                    reduce_y[o][k][part].start()
            if part in REDUCE_CROSS:
                reduce_z[o][1][part].start()

    def join(o, part):
        cut = cuts[part]
        for k in order:
            if k > 1 or (k == 1 and part not in REDUCE_CROSS):
                reduce_y[o][k][part].wait_recv()
                total = y_keep[o, k, :, cut] + y_recv[o, k, :, cut].astype(jnp.float32)
                z_send[o, k, :, cut] = total.astype(jnp.bfloat16)
                reduce_z[o][k][part].start()

    def join_cross(o, part):
        if part in REDUCE_CROSS:
            cut = cuts[part]
            reduce_cross[o][part].wait_recv()
            total = cross_keep[o, :, cut] + cross_recv[o, :, cut].astype(jnp.float32)
            y_send[o, 0, :, cut] = total.astype(jnp.bfloat16)
            reduce_y[o][0][part].start()

    def join_own(o, part):
        cut = cuts[part]
        reduce_y[o][0][part].wait_recv()
        own_sum[o, :, cut] = y_keep[o, 0, :, cut] + y_recv[o, 0, :, cut].astype(jnp.float32)

    arrived(0)
    first = contract(0, segment)
    relays([(2, 3)], [])
    arrived(1)
    pre = contract(1, 0)
    gate = sigmoid(pre)
    slope[...] = gate * (1.0 + pre * (1.0 - gate))
    expand(first * sigmoid(first) * (1.0 - later) + first * slope[...] * later, segment, 0)
    arrived(2)
    last = contract(2, 1 - segment)
    expand(last * slope[...] * (1.0 - later) + last * sigmoid(last) * later, 1 - segment, 1)
    for o in range(2):
        for part in parts:
            join(o, part)
        for part in parts:
            join_cross(o, part)
    for o in range(2):
        for part in parts:
            join_own(o, part)
    for o in range(2):
        whole(planes - 1, reduces, land_back_z[o][0]).wait_recv()
        total = own_sum[o]
        for k in range(1, planes):
            total = total + z_recv[o, k].astype(jnp.float32)
        sums[segment if o == 0 else 1 - segment] = total.astype(jnp.bfloat16)
    request.wait_send()
    give_in.wait_send()
    give_out.wait_send()
    whole(5 * planes - 1, gathers, land_y[0][0]).wait_send()
    whole(4 * planes - 2, reduces, land_y[0][0]).wait_send()

    @pl.when(inner)
    def _():
        whole(6, inners, land_y[0][0]).wait_send()


def scatter_kernel(chunk, sums, places, gate_wide, out_f, out_b):
    width = out_f.shape[1]
    column = lax.broadcasted_iota(jnp.int32, places.shape[1:], 1)
    gate = gate_wide[:, 0:1]
    tail = chunk // CAP

    def product(i, chosen, columns):
        return jnp.dot(chosen.astype(jnp.bfloat16), sums[i, :, columns], preferred_element_type=jnp.float32)

    for i, out in enumerate([out_f, out_b]):
        placed = places[i].astype(jnp.float32)

        def put(columns, value):
            out[:, columns] = (value * gate if i == 0 else value).astype(jnp.bfloat16)

        for q in range(THIRDS):
            inside = (column >= CAP * q) & (column < CAP * (q + 1))
            put(slice(q * chunk, (q + 1) * chunk), product(i, jnp.where(inside, placed, 0.0), slice(0, chunk)))
        put(
            slice(THIRDS * chunk, width),
            sum(
                product(
                    i,
                    jnp.where(column == BLOCK - 1, placed[:, slot : slot + 1], 0.0),
                    slice(slot * tail, (slot + 1) * tail),
                )
                for slot in range(CAP)
            ),
        )


def exchange(planes, handoff, saved_inputs, cotangent, ids_forward, gates_forward, ids_backward, gates_backward, weight_in, weight_out):
    rows, width = handoff.shape[1:]
    hidden = weight_out.shape[1]
    chunk = width // BLOCK * CAP
    bf16, f32 = jnp.bfloat16, jnp.float32
    landings = 3 + PARTS * 5 * planes + 5 + PARTS * 5
    vmem = pl.BlockSpec(memory_space=pltpu.VMEM)
    hbm = pl.BlockSpec(memory_space=pl.ANY)
    sums, places, gate_wide = pl.pallas_call(
        functools.partial(exchange_kernel, planes, chunk),
        out_shape=[
            pltpu.VMEM((2, BLOCK, chunk), bf16),
            pltpu.VMEM((2, rows, BLOCK), bf16),
            pltpu.VMEM((rows, LANES), f32),
        ],
        in_specs=[hbm] * 9,
        out_specs=[vmem] * 3,
        scratch_shapes=[
            pltpu.VMEM((rows, width), bf16),
            pltpu.VMEM((rows, width), bf16),
            pltpu.VMEM((2, width, 2 * hidden), bf16),
            pltpu.VMEM((2, 2 * hidden, width), bf16),
            pltpu.VMEM((6 * planes, BLOCK, chunk), bf16),
            pltpu.VMEM((BLOCK, LANES), f32),
            pltpu.VMEM((BLOCK, LANES), f32),
            pltpu.VMEM((BLOCK, chunk), bf16),
            pltpu.VMEM((2 * planes * BLOCK, 2 * hidden), f32),
            pltpu.VMEM((2, planes, BLOCK, chunk), bf16),
            pltpu.VMEM((2, planes, BLOCK, chunk), f32),
            pltpu.VMEM((2, planes, BLOCK, chunk), bf16),
            pltpu.VMEM((2, BLOCK, chunk), f32),
            pltpu.VMEM((2, BLOCK, chunk), bf16),
            pltpu.VMEM((2, planes, BLOCK, chunk), bf16),
            pltpu.VMEM((2, planes, BLOCK, chunk), bf16),
            pltpu.VMEM((2, BLOCK, chunk), f32),
            pltpu.VMEM((2, rows), jnp.int32),
            pltpu.VMEM((2, rows), f32),
            pltpu.VMEM((2, rows), jnp.int32),
            pltpu.VMEM((2, rows), f32),
            pltpu.SemaphoreType.DMA((8,)),
            pltpu.SemaphoreType.DMA((6,)),
            pltpu.SemaphoreType.DMA((landings,)),
        ],
        compiler_params=pltpu.CompilerParams(
            collective_id=0, has_side_effects=True
        ),
    )(
        ids_forward[0].T,
        gates_forward[0].T,
        ids_backward[0].T,
        gates_backward[0].T,
        handoff[0],
        saved_inputs[0],
        cotangent[0],
        weight_in[0],
        weight_out[0],
    )
    mixed, grads = pl.pallas_call(
        functools.partial(scatter_kernel, chunk),
        out_shape=[jax.ShapeDtypeStruct((rows, width), bf16)] * 2,
        in_specs=[vmem] * 3,
        out_specs=[vmem] * 2,
    )(*[pltpu.with_memory_space_constraint(x, pltpu.VMEM) for x in (sums, places, gate_wide)])
    return (mixed[None], grads[None])


def device_body(mesh):
    segments, experts = mesh.shape["segment"], mesh.shape["expert"]
    planes = experts // 4
    if segments == 2 and experts == GROUP and planes == 4:
        return functools.partial(exchange, planes)
    return per_device


def solution(mesh):
    return jax.shard_map(
        device_body(mesh),
        mesh=mesh,
        in_specs=(
            P("segment", "expert", None),
            P("segment", "expert", None),
            P("segment", "expert", None),
            P("segment", "expert", None),
            P("segment", "expert", None),
            P("segment", "expert", None),
            P("segment", "expert", None),
            P("segment", None, "expert"),
            P("segment", "expert", None),
        ),
        out_specs=(P("segment", "expert", None), P("segment", "expert", None)),
        check_vma=False,
    )
```

```python
import functools

import jax
import jax.numpy as jnp
from jax import lax
from jax.experimental import pallas as pl
from jax.experimental.pallas import tpu as pltpu
from jax.sharding import PartitionSpec as P

GROUP = 16
CAP = 5


def shifted(block, axis, distance):
    devices = range(lax.axis_size(axis))
    route = [(i - distance, i) for i in devices if i - distance in devices]
    return lax.ppermute(block, axis, route)


def slot_tables(expert_ids, gate_values, experts):
    row_count = expert_ids.shape[0]
    flat_ids = expert_ids.reshape(row_count * 2)
    window = jnp.arange(experts, dtype=jnp.int32)
    member = (flat_ids[None, :] == window[:, None]).astype(jnp.int32)
    before = jnp.cumsum(member, axis=1, dtype=jnp.int32) - member
    positions = jnp.arange(CAP, dtype=jnp.int32)
    picked_slots = (
        member[:, None, :] * (before[:, None, :] == positions[None, :, None]).astype(jnp.int32)
    ).astype(jnp.float32)
    picked_slots = picked_slots.reshape(experts * CAP, row_count, 2)
    select = jnp.sum(picked_slots, axis=2)
    weighted = jnp.sum(picked_slots * gate_values[None, :, :], axis=2)
    return (select, weighted)


def pack_direct(stacked, groups):
    stacks = stacked.shape[0]
    feature_width = stacked.shape[2]
    shaped = stacked.reshape(stacks, groups, 1, CAP, feature_width)
    spread_out = jnp.broadcast_to(shaped, (stacks, groups, GROUP, CAP, feature_width))
    return spread_out.reshape(stacks, groups * GROUP, CAP, feature_width)


def expert_forward(arriving, local_in, local_out):
    feature_width = arriving.shape[-1]
    preact = jnp.dot(
        arriving.reshape(-1, feature_width), local_in, preferred_element_type=jnp.float32
    )
    hidden = jax.nn.silu(preact).astype(jnp.bfloat16)
    partial_out = jnp.dot(hidden, local_out, preferred_element_type=jnp.float32).astype(
        jnp.bfloat16
    )
    return partial_out.reshape(arriving.shape)


def expert_backward(row_part, grad_part, local_in, local_out):
    feature_width = row_part.shape[-1]
    preact = jnp.dot(
        row_part.reshape(-1, feature_width), local_in, preferred_element_type=jnp.float32
    )
    sigmoid_v = jax.nn.sigmoid(preact)
    slope_v = sigmoid_v * (1.0 + preact * (1.0 - sigmoid_v))
    grad_hidden = jnp.einsum(
        "rd,hd->rh",
        grad_part.reshape(-1, feature_width),
        local_out,
        preferred_element_type=jnp.float32,
    )
    grad_pre = (grad_hidden * slope_v).astype(jnp.bfloat16)
    partial_grad = jnp.einsum(
        "rh,dh->rd", grad_pre, local_in, preferred_element_type=jnp.float32
    ).astype(jnp.bfloat16)
    return partial_grad.reshape(row_part.shape)


def gather_groups(returned, groups):
    feature_width = returned.shape[-1]
    summed = jnp.sum(
        returned.reshape(groups, GROUP, CAP, feature_width).astype(jnp.float32), axis=1
    )
    return summed.reshape(groups * CAP, feature_width)


def per_device(
    handoff,
    saved_inputs,
    cotangent,
    ids_forward,
    gates_forward,
    ids_backward,
    gates_backward,
    weight_in,
    weight_out,
):
    highest = lax.Precision.HIGHEST
    groups = lax.axis_size("expert") // GROUP
    segment_index = lax.axis_index("segment")
    last_segment = lax.axis_size("segment") - 1
    arrived = shifted(handoff, "segment", 1)
    inputs = jnp.where(segment_index == 0, handoff, arrived)[0]
    returned = shifted(cotangent, "segment", -1)
    upstream = jnp.where(segment_index == last_segment, cotangent, returned)[0]
    local_in = weight_in[0]
    local_out = weight_out[0]
    select_f, weigh_f = slot_tables(ids_forward[0], gates_forward[0], groups)
    picked = jnp.dot(
        select_f.astype(jnp.bfloat16), inputs, preferred_element_type=jnp.float32
    ).astype(jnp.bfloat16)
    select_b, weigh_b = slot_tables(ids_backward[0], gates_backward[0], groups)
    rows_back = jnp.dot(
        select_b.astype(jnp.bfloat16), saved_inputs[0], preferred_element_type=jnp.float32
    ).astype(jnp.bfloat16)
    grads_out = jnp.dot(
        weigh_b, upstream.astype(jnp.float32), precision=highest, preferred_element_type=jnp.float32
    ).astype(jnp.bfloat16)
    backward_stack = jnp.stack([rows_back, grads_out])
    arriving_f = lax.all_to_all(
        pack_direct(picked[None], groups), "expert", split_axis=1, concat_axis=1, tiled=True
    )
    arriving_b = lax.all_to_all(
        pack_direct(backward_stack, groups), "expert", split_axis=1, concat_axis=1, tiled=True
    )
    partial_f = expert_forward(arriving_f[0], local_in, local_out)
    back_f = lax.all_to_all(partial_f, "expert", split_axis=0, concat_axis=0, tiled=True)
    combined = gather_groups(back_f, groups)
    expert_mix = jnp.dot(
        weigh_f.T, combined, precision=highest, preferred_element_type=jnp.float32
    ).astype(jnp.bfloat16)
    partial_b = expert_backward(arriving_b[0], arriving_b[1], local_in, local_out)
    back_b = lax.all_to_all(partial_b, "expert", split_axis=0, concat_axis=0, tiled=True)
    slot_grads = gather_groups(back_b, groups)
    input_grads = jnp.dot(
        select_b.T, slot_grads, precision=highest, preferred_element_type=jnp.float32
    ).astype(jnp.bfloat16)
    return (expert_mix[None], input_grads[None])


MESH = pl.DeviceIdType.MESH
BLOCK = 16
THIRDS = 3
PARTS = 2
LANES = 128
GATHER_CROSS = (0,)
REDUCE_CROSS = (0, 1)
CORNER = (1, 2)


def flipped(position, mask):
    bit = 1
    while bit <= mask:
        if mask & bit:
            position = position + bit * (1 - 2 * ((position // bit) % 2))
        bit *= 2
    return position


def exchange_kernel(
    planes,
    chunk,
    ids_f_hbm,
    gates_f_hbm,
    ids_b_hbm,
    gates_b_hbm,
    handoff,
    saved,
    cotangent,
    weight_in,
    weight_out,
    sums,
    places,
    gate_wide,
    rows_x,
    rows_s,
    w_first,
    w_second,
    blocks,
    req_send,
    req_recv,
    late_send,
    slope,
    y_send,
    y_keep,
    y_recv,
    cross_keep,
    cross_recv,
    z_send,
    z_recv,
    own_sum,
    ids_f,
    gates_f,
    ids_b,
    gates_b,
    local_sem,
    send_sem,
    recv_sem,
):
    segment = lax.axis_index("segment")
    expert = lax.axis_index("expert")
    row_count, width = rows_x.shape
    hidden = weight_out.shape[0]
    tail = chunk // CAP
    rest = THIRDS * chunk

    def at_expert(mask):
        return {"expert": flipped(expert, mask)}

    def at_other(k):
        return {"segment": 1 - segment, "expert": flipped(expert, 4 * k)}

    sibling = at_expert(1)
    across = at_expert(2)
    mates = [None] + [at_expert(4 * k) for k in range(1, planes)]
    others = [at_other(k) for k in range(planes)]

    barrier = pltpu.get_barrier_semaphore()
    plane = expert // 4
    inner = (plane > 0) & (plane < planes - 1)
    partners = [across, sibling, others[0]] + mates[1 : planes - 1]
    for partner in partners:
        pl.semaphore_signal(barrier, inc=1, device_id=partner, device_id_type=MESH)

    @pl.when(inner)
    def _():
        pl.semaphore_signal(barrier, inc=1, device_id=mates[-1], device_id_type=MESH)


    tables = [
        pltpu.make_async_copy(source, target, local_sem.at[4 + i])
        for i, (source, target) in enumerate(
            [(ids_f_hbm, ids_f), (gates_f_hbm, gates_f), (ids_b_hbm, ids_b), (gates_b_hbm, gates_b)]
        )
    ]
    for table_copy in tables:
        table_copy.start()

    @pl.when(segment == 0)
    def _():
        pltpu.make_async_copy(handoff, rows_x, local_sem.at[0]).start()

    @pl.when(segment != 0)
    def _():
        pltpu.make_async_copy(cotangent, rows_x, local_sem.at[0]).start()

    load_x = pltpu.make_async_copy(handoff, rows_x, local_sem.at[0])
    load_s = pltpu.make_async_copy(saved, rows_s, local_sem.at[1])
    load_in = pltpu.make_async_copy(weight_in, w_first.at[0, :, 0:hidden], local_sem.at[2])
    load_out = pltpu.make_async_copy(weight_out, w_second.at[0, 0:hidden, :], local_sem.at[3])
    load_s.start()
    load_in.start()
    load_out.start()

    count = [0]

    def landing():
        count[0] += 1
        return recv_sem.at[count[0] - 1]

    def remote(source, target, device, leaving, arriving):
        return pltpu.make_async_remote_copy(
            src_ref=source,
            dst_ref=target,
            send_sem=leaving,
            recv_sem=arriving,
            device_id=device,
            device_id_type=MESH,
        )

    def start_inner(copies):
        @pl.when(inner)
        def _():
            for copy in copies:
                copy.start()

    parts = range(PARTS)
    edges = [CAP * i // PARTS for i in range(PARTS + 1)]
    cuts = [slice(tail * low, tail * high) for low, high in zip(edges[:-1], edges[1:])]

    request = remote(req_send, req_recv, others[0], send_sem.at[0], landing())
    give_in = remote(weight_in, w_first.at[0, :, hidden : 2 * hidden], sibling, send_sem.at[1], landing())
    give_out = remote(weight_out, w_second.at[0, hidden : 2 * hidden, :], sibling, send_sem.at[2], landing())

    def ship(source, target, device, leaving, arriving):
        return [
            remote(source.at[:, cut], target.at[:, cut], device, leaving, arriving[part])
            for part, cut in enumerate(cuts)
        ]

    def block(kind, k, side=0):
        return blocks.at[(kind * planes + k) * 2 + side]

    far = planes - 1
    gathers, inners, reduces, fars, corners = [send_sem.at[i] for i in range(3, 8)]
    land_z = [[[landing() for part in parts] for k in range(planes)] for kind in range(3)]
    land_y = [[landing()] * PARTS for kind in range(3)]
    land_near = [[landing() for part in parts] for kind in range(3)]
    land_cross = [[landing() for part in parts] for o in range(2)]
    land_back_y = [[[landing() for part in parts] for k in range(planes)] for o in range(2)]
    land_back_z = [[landing()] * PARTS for o in range(2)]
    gather_z = []
    for kind in range(3):
        sources = [late_send if kind == 2 else block(kind, 0)] * planes
        targets = others if kind == 2 else mates
        gather_z.append(
            [
                None
                if targets[k] is None
                else ship(sources[k], block(kind, k), targets[k], inners if k == far else gathers, land_z[kind][k])
                for k in range(planes)
            ]
        )
    forward_z = [ship(block(kind, 2), block(kind, far), mates[1], inners, land_z[kind][far]) for kind in range(3)]
    gather_y = [
        [
            ship(block(kind, k), block(kind, k, 1), across, fars if k == far else gathers, land_y[kind] if k else land_near[kind])
            for k in range(planes)
        ]
        for kind in range(3)
    ]
    corner_z = [
        ship(block(kind, 2), block(kind, far, 1), at_expert(6), corners, land_y[kind]) for kind in range(3)
    ]
    gather_cross = [
        ship(block(kind, 0, 1), block(kind, 1, 1), mates[1], gathers, land_y[kind]) for kind in range(3)
    ]
    reduce_cross = [ship(y_send.at[o, 1], cross_recv.at[o], mates[1], reduces, land_cross[o]) for o in range(2)]
    reduce_y = [
        [ship(y_send.at[o, k], y_recv.at[o, k], across, reduces, land_back_y[o][k]) for k in range(planes)]
        for o in range(2)
    ]
    reduce_z = [
        [None] + [ship(z_send.at[o, k], z_recv.at[o, k], mates[k], reduces, land_back_z[o]) for k in range(1, planes)]
        for o in range(2)
    ]

    def whole(number, leaving, arriving):
        return remote(blocks.at[0:number], blocks.at[0:number], across, leaving, arriving)

    for table_copy in tables:
        table_copy.wait()
    earlier = jnp.where(
        lax.broadcasted_iota(jnp.int32, (row_count, row_count), 0)
        < lax.broadcasted_iota(jnp.int32, (row_count, row_count), 1),
        1.0,
        0.0,
    ).astype(jnp.bfloat16)
    block_row = lax.broadcasted_iota(jnp.int32, (BLOCK, row_count), 0)
    third = sum((block_row >= CAP * q).astype(jnp.int32) for q in range(1, THIRDS + 1))
    slot = block_row - CAP * third

    def ranks(ids, gates):
        first, second = ids[0:1, :] == 0, ids[1:2, :] == 0
        member = jnp.where(first | second, 1.0, 0.0)
        gate = jnp.where(first, gates[0:1, :], 0.0) + jnp.where(second, gates[1:2, :], 0.0)
        wide = jnp.broadcast_to(member, (BLOCK, row_count))
        rank = jnp.dot(wide.astype(jnp.bfloat16), earlier, preferred_element_type=jnp.float32)
        placed = jnp.where((slot == rank.astype(jnp.int32)) & (third < THIRDS), wide, 0.0)
        return placed, gate

    placed_f, gate_f = ranks(ids_f, gates_f)
    placed_b, gate_b = ranks(ids_b, gates_b)
    later = (segment * jnp.ones((), jnp.int32)).astype(jnp.float32)
    scaled_b = placed_b * gate_b
    asked = scaled_b * (1.0 - later) + placed_f * later
    mine = placed_f * (1.0 - later) + scaled_b * later
    req_send[...] = jnp.concatenate([asked, jnp.zeros((BLOCK, LANES - row_count), jnp.float32)], axis=1)

    @pl.when(inner)
    def _():
        pl.semaphore_wait(barrier, len(partners) + 1)

    @pl.when(jnp.logical_not(inner))
    def _():
        pl.semaphore_wait(barrier, len(partners))

    request.start()

    def pick(weights, rows_ref, target):
        ending = jnp.concatenate(
            [jnp.where(block_row == BLOCK - 1, weights[i : i + 1, :], 0.0) for i in range(CAP)], axis=0
        )

        def product(chosen, columns):
            return jnp.dot(
                jnp.where(chosen, 1.0, 0.0).astype(jnp.bfloat16),
                rows_ref[:, columns],
                preferred_element_type=jnp.float32,
            )

        scale = jnp.sum(weights, axis=1, keepdims=True)
        chosen = [(weights != 0.0) & (third == q) for q in range(THIRDS)]
        last = product(ending != 0.0, slice(rest, width)) * jnp.sum(ending, axis=1, keepdims=True)
        for i in range(CAP):
            total = sum(
                product(chosen[q], slice(q * chunk + i * tail, q * chunk + (i + 1) * tail)) for q in range(THIRDS)
            )
            value = total * scale + last[i * BLOCK : (i + 1) * BLOCK]
            target[:, i * tail : (i + 1) * tail] = value.astype(jnp.bfloat16)

    def spread(kind):
        for part in parts:
            gather_y[kind][0][part].start()
            for k in range(1, far):
                gather_z[kind][k][part].start()
        start_inner(gather_z[kind][far])

    load_x.wait()
    pick(mine, rows_x, block(0, 0))
    spread(0)
    load_s.wait()
    pick(placed_b, rows_s, block(1, 0))
    spread(1)
    give_in.start()
    give_out.start()
    turn = 512 if width % 512 == 0 else LANES

    def transpose(low, share=0, shares=1):
        half = slice(low, low + hidden)

        def step(number, carry):
            piece = pl.ds(pl.multiple_of(number * turn, turn), turn)
            w_first[1, piece, half] = w_second[0, half, piece].T
            w_second[1, half, piece] = w_first[0, piece, half].T
            return carry

        steps = width // turn
        lax.fori_loop(steps * share // shares, steps * (share + 1) // shares, step, 0)

    load_in.wait()
    load_out.wait()
    transpose(0)
    request.wait_recv()
    pick(req_recv[:, 0:row_count], rows_x, late_send)
    for part in parts:
        for k in range(far):
            gather_z[2][k][part].start()
    start_inner(gather_z[2][far])

    def relay(kind, k, corner=False):
        for part in parts:
            gather_z[kind][k][part].wait_recv()
            if k == 2:
                start_inner([forward_z[kind][part]] + ([corner_z[kind][part]] if kind in CORNER else []))
            if not corner and (k != 1 or part not in GATHER_CROSS):
                gather_y[kind][k][part].start()

    def cross(kind):
        for part in parts:
            gather_y[kind][0][part].wait_recv()
            if part in GATHER_CROSS:
                gather_cross[kind][part].start()

    def relays(outer_order, inner_order):
        @pl.when(inner)
        def _():
            for kind, k in inner_order:
                relay(kind, k)

        @pl.when(jnp.logical_not(inner))
        def _():
            for kind, k in outer_order:
                relay(kind, k, k == far and kind in CORNER)

    relays([(0, 1), (0, 2), (1, 1)], [(0, 1), (0, 2), (0, 3), (1, 1)])
    cross(0)
    cross(1)
    relays([(2, 0)], [(1, 2), (2, 0), (1, 3)])
    give_in.wait_recv()
    give_out.wait_recv()
    transpose(hidden, 0, 2)
    relays([(1, 2), (2, 1)], [(2, 1)])
    transpose(hidden, 1, 2)
    relays([(0, 3), (2, 2)], [(2, 2), (2, 3)])
    cross(2)
    unit = jnp.where(
        lax.broadcasted_iota(jnp.int32, (row_count, row_count), 0)
        == lax.broadcasted_iota(jnp.int32, (row_count, row_count), 1),
        1.0,
        0.0,
    )
    by_row = (((1,), (1,)), ((), ()))
    for i, placed in enumerate([placed_f, placed_b]):
        places[i] = lax.dot_general(
            unit.astype(jnp.bfloat16),
            placed.astype(jnp.bfloat16),
            by_row,
            preferred_element_type=jnp.float32,
        ).astype(jnp.bfloat16)
    gate_wide[...] = lax.dot_general(
        unit,
        jnp.broadcast_to(gate_f, (LANES, row_count)),
        by_row,
        precision=lax.Precision.HIGHEST,
        preferred_element_type=jnp.float32,
    )

    batch = 2 * planes * BLOCK
    place = lax.broadcasted_iota(jnp.int32, (batch, 2 * hidden), 0) % BLOCK

    def arrived(kind):
        whole(planes - 1, gathers, land_y[kind][0]).wait_recv()

    def contract(kind, side):
        gathered = blocks[2 * planes * kind : 2 * planes * (kind + 1)].reshape(batch, chunk)

        def product(columns, rows):
            return jnp.dot(gathered[:, columns], w_first[side, rows, :], preferred_element_type=jnp.float32)

        value = product(slice(0, chunk), slice(0, chunk))
        for q in range(1, THIRDS):
            value = value + pltpu.roll(
                product(slice(0, chunk), slice(q * chunk, (q + 1) * chunk)), batch - CAP * q, 0
            )
        for i in range(CAP):
            last = product(slice(i * tail, (i + 1) * tail), slice(rest, width))
            value = value + jnp.where(place == i, pltpu.roll(last, batch - (BLOCK - 1 - i), 0), 0.0)
        return value

    def sigmoid(value):
        return 1.0 / (1.0 + jnp.exp(-value))

    order = [k for k in range(planes - 1, -1, -1)]

    def expand(value, side, o):
        value = jnp.where(place < CAP, value, 0.0)
        left = [value.astype(jnp.bfloat16)]
        left += [pltpu.roll(value, CAP * q, 0).astype(jnp.bfloat16) for q in range(1, THIRDS)]
        for part in parts:
            for i in range(edges[part], edges[part + 1]):
                piece = slice(i * tail, (i + 1) * tail)
                total = sum(
                    jnp.dot(
                        left[q],
                        w_second[side, :, q * chunk + i * tail : q * chunk + (i + 1) * tail],
                        preferred_element_type=jnp.float32,
                    )
                    for q in range(THIRDS)
                )
                last = jnp.where(place == BLOCK - 1, pltpu.roll(value, BLOCK - 1 - i, 0), 0.0)
                total = total + jnp.dot(
                    last.astype(jnp.bfloat16), w_second[side, :, rest:width], preferred_element_type=jnp.float32
                )
                total = total.reshape(planes, 2, BLOCK, tail)
                y_keep[o, :, :, piece] = total[:, 0]
                y_send[o, 1:planes, :, piece] = total[1:planes, 1].astype(jnp.bfloat16)
                if part in REDUCE_CROSS:
                    cross_keep[o, :, piece] = total[0, 1]
                    z_send[o, 1, :, piece] = total[1, 0].astype(jnp.bfloat16)
                else:
                    y_send[o, 0, :, piece] = total[0, 1].astype(jnp.bfloat16)
            if part in REDUCE_CROSS:
                reduce_cross[o][part].start()
            for k in order:
                if k > 1 or part not in REDUCE_CROSS:
                    reduce_y[o][k][part].start()
            if part in REDUCE_CROSS:
                reduce_z[o][1][part].start()

    def join(o, part):
        cut = cuts[part]
        for k in order:
            if k > 1 or (k == 1 and part not in REDUCE_CROSS):
                reduce_y[o][k][part].wait_recv()
                total = y_keep[o, k, :, cut] + y_recv[o, k, :, cut].astype(jnp.float32)
                z_send[o, k, :, cut] = total.astype(jnp.bfloat16)
                reduce_z[o][k][part].start()

    def join_cross(o, part):
        if part in REDUCE_CROSS:
            cut = cuts[part]
            reduce_cross[o][part].wait_recv()
            total = cross_keep[o, :, cut] + cross_recv[o, :, cut].astype(jnp.float32)
            y_send[o, 0, :, cut] = total.astype(jnp.bfloat16)
            reduce_y[o][0][part].start()

    def join_own(o, part):
        cut = cuts[part]
        reduce_y[o][0][part].wait_recv()
        own_sum[o, :, cut] = y_keep[o, 0, :, cut] + y_recv[o, 0, :, cut].astype(jnp.float32)

    arrived(0)
    first = contract(0, segment)
    relays([(1, 3)], [])
    arrived(1)
    pre = contract(1, 0)
    gate = sigmoid(pre)
    slope[...] = gate * (1.0 + pre * (1.0 - gate))
    expand(first * sigmoid(first) * (1.0 - later) + first * slope[...] * later, segment, 0)
    relays([(2, 3)], [])
    arrived(2)
    last = contract(2, 1 - segment)
    expand(last * slope[...] * (1.0 - later) + last * sigmoid(last) * later, 1 - segment, 1)
    for o in range(2):
        for part in parts:
            join(o, part)
        for part in parts:
            join_cross(o, part)
    for o in range(2):
        for part in parts:
            join_own(o, part)
    for o in range(2):
        whole(planes - 1, reduces, land_back_z[o][0]).wait_recv()
        total = own_sum[o]
        for k in range(1, planes):
            total = total + z_recv[o, k].astype(jnp.float32)
        sums[segment if o == 0 else 1 - segment] = total.astype(jnp.bfloat16)
    request.wait_send()
    give_in.wait_send()
    give_out.wait_send()
    whole(5 * planes - 4, gathers, land_y[0][0]).wait_send()
    whole(4 * planes - 2, reduces, land_y[0][0]).wait_send()

    @pl.when(inner)
    def _():
        whole(6, inners, land_y[0][0]).wait_send()
        whole(3, fars, land_y[0][0]).wait_send()
        if CORNER:
            whole(len(CORNER), corners, land_y[0][0]).wait_send()

    @pl.when(jnp.logical_not(inner))
    def _():
        if len(CORNER) < 3:
            whole(3 - len(CORNER), fars, land_y[0][0]).wait_send()


def scatter_kernel(chunk, sums, places, gate_wide, out_f, out_b):
    width = out_f.shape[1]
    column = lax.broadcasted_iota(jnp.int32, places.shape[1:], 1)
    gate = gate_wide[:, 0:1]
    tail = chunk // CAP

    def product(i, chosen, columns):
        return jnp.dot(chosen.astype(jnp.bfloat16), sums[i, :, columns], preferred_element_type=jnp.float32)

    for i, out in enumerate([out_f, out_b]):
        placed = places[i].astype(jnp.float32)

        def put(columns, value):
            out[:, columns] = (value * gate if i == 0 else value).astype(jnp.bfloat16)

        for q in range(THIRDS):
            inside = (column >= CAP * q) & (column < CAP * (q + 1))
            put(slice(q * chunk, (q + 1) * chunk), product(i, jnp.where(inside, placed, 0.0), slice(0, chunk)))
        put(
            slice(THIRDS * chunk, width),
            sum(
                product(
                    i,
                    jnp.where(column == BLOCK - 1, placed[:, slot : slot + 1], 0.0),
                    slice(slot * tail, (slot + 1) * tail),
                )
                for slot in range(CAP)
            ),
        )


def exchange(planes, handoff, saved_inputs, cotangent, ids_forward, gates_forward, ids_backward, gates_backward, weight_in, weight_out):
    rows, width = handoff.shape[1:]
    hidden = weight_out.shape[1]
    chunk = width // BLOCK * CAP
    bf16, f32 = jnp.bfloat16, jnp.float32
    landings = 3 + PARTS * 5 * planes + 5 + PARTS * 5
    vmem = pl.BlockSpec(memory_space=pltpu.VMEM)
    hbm = pl.BlockSpec(memory_space=pl.ANY)
    sums, places, gate_wide = pl.pallas_call(
        functools.partial(exchange_kernel, planes, chunk),
        out_shape=[
            pltpu.VMEM((2, BLOCK, chunk), bf16),
            pltpu.VMEM((2, rows, BLOCK), bf16),
            pltpu.VMEM((rows, LANES), f32),
        ],
        in_specs=[hbm] * 9,
        out_specs=[vmem] * 3,
        scratch_shapes=[
            pltpu.VMEM((rows, width), bf16),
            pltpu.VMEM((rows, width), bf16),
            pltpu.VMEM((2, width, 2 * hidden), bf16),
            pltpu.VMEM((2, 2 * hidden, width), bf16),
            pltpu.VMEM((6 * planes, BLOCK, chunk), bf16),
            pltpu.VMEM((BLOCK, LANES), f32),
            pltpu.VMEM((BLOCK, LANES), f32),
            pltpu.VMEM((BLOCK, chunk), bf16),
            pltpu.VMEM((2 * planes * BLOCK, 2 * hidden), f32),
            pltpu.VMEM((2, planes, BLOCK, chunk), bf16),
            pltpu.VMEM((2, planes, BLOCK, chunk), f32),
            pltpu.VMEM((2, planes, BLOCK, chunk), bf16),
            pltpu.VMEM((2, BLOCK, chunk), f32),
            pltpu.VMEM((2, BLOCK, chunk), bf16),
            pltpu.VMEM((2, planes, BLOCK, chunk), bf16),
            pltpu.VMEM((2, planes, BLOCK, chunk), bf16),
            pltpu.VMEM((2, BLOCK, chunk), f32),
            pltpu.VMEM((2, rows), jnp.int32),
            pltpu.VMEM((2, rows), f32),
            pltpu.VMEM((2, rows), jnp.int32),
            pltpu.VMEM((2, rows), f32),
            pltpu.SemaphoreType.DMA((8,)),
            pltpu.SemaphoreType.DMA((8,)),
            pltpu.SemaphoreType.DMA((landings,)),
        ],
        compiler_params=pltpu.CompilerParams(
            collective_id=0, has_side_effects=True
        ),
    )(
        ids_forward[0].T,
        gates_forward[0].T,
        ids_backward[0].T,
        gates_backward[0].T,
        handoff[0],
        saved_inputs[0],
        cotangent[0],
        weight_in[0],
        weight_out[0],
    )
    mixed, grads = pl.pallas_call(
        functools.partial(scatter_kernel, chunk),
        out_shape=[jax.ShapeDtypeStruct((rows, width), bf16)] * 2,
        in_specs=[vmem] * 3,
        out_specs=[vmem] * 2,
    )(*[pltpu.with_memory_space_constraint(x, pltpu.VMEM) for x in (sums, places, gate_wide)])
    return (mixed[None], grads[None])


def device_body(mesh):
    segments, experts = mesh.shape["segment"], mesh.shape["expert"]
    planes = experts // 4
    if segments == 2 and experts == GROUP and planes == 4:
        return functools.partial(exchange, planes)
    return per_device


def solution(mesh):
    return jax.shard_map(
        device_body(mesh),
        mesh=mesh,
        in_specs=(
            P("segment", "expert", None),
            P("segment", "expert", None),
            P("segment", "expert", None),
            P("segment", "expert", None),
            P("segment", "expert", None),
            P("segment", "expert", None),
            P("segment", "expert", None),
            P("segment", None, "expert"),
            P("segment", "expert", None),
        ),
        out_specs=(P("segment", "expert", None), P("segment", "expert", None)),
        check_vma=False,
    )
```

```python
import functools

import jax
import jax.numpy as jnp
from jax import lax
from jax.experimental import pallas as pl
from jax.experimental.pallas import tpu as pltpu
from jax.sharding import PartitionSpec as P

GROUP = 16
CAP = 5


def shifted(block, axis, distance):
    devices = range(lax.axis_size(axis))
    route = [(i - distance, i) for i in devices if i - distance in devices]
    return lax.ppermute(block, axis, route)


def slot_tables(expert_ids, gate_values, experts):
    row_count = expert_ids.shape[0]
    flat_ids = expert_ids.reshape(row_count * 2)
    window = jnp.arange(experts, dtype=jnp.int32)
    member = (flat_ids[None, :] == window[:, None]).astype(jnp.int32)
    before = jnp.cumsum(member, axis=1, dtype=jnp.int32) - member
    positions = jnp.arange(CAP, dtype=jnp.int32)
    picked_slots = (
        member[:, None, :] * (before[:, None, :] == positions[None, :, None]).astype(jnp.int32)
    ).astype(jnp.float32)
    picked_slots = picked_slots.reshape(experts * CAP, row_count, 2)
    select = jnp.sum(picked_slots, axis=2)
    weighted = jnp.sum(picked_slots * gate_values[None, :, :], axis=2)
    return (select, weighted)


def pack_direct(stacked, groups):
    stacks = stacked.shape[0]
    feature_width = stacked.shape[2]
    shaped = stacked.reshape(stacks, groups, 1, CAP, feature_width)
    spread_out = jnp.broadcast_to(shaped, (stacks, groups, GROUP, CAP, feature_width))
    return spread_out.reshape(stacks, groups * GROUP, CAP, feature_width)


def expert_forward(arriving, local_in, local_out):
    feature_width = arriving.shape[-1]
    preact = jnp.dot(
        arriving.reshape(-1, feature_width), local_in, preferred_element_type=jnp.float32
    )
    hidden = jax.nn.silu(preact).astype(jnp.bfloat16)
    partial_out = jnp.dot(hidden, local_out, preferred_element_type=jnp.float32).astype(
        jnp.bfloat16
    )
    return partial_out.reshape(arriving.shape)


def expert_backward(row_part, grad_part, local_in, local_out):
    feature_width = row_part.shape[-1]
    preact = jnp.dot(
        row_part.reshape(-1, feature_width), local_in, preferred_element_type=jnp.float32
    )
    sigmoid_v = jax.nn.sigmoid(preact)
    slope_v = sigmoid_v * (1.0 + preact * (1.0 - sigmoid_v))
    grad_hidden = jnp.einsum(
        "rd,hd->rh",
        grad_part.reshape(-1, feature_width),
        local_out,
        preferred_element_type=jnp.float32,
    )
    grad_pre = (grad_hidden * slope_v).astype(jnp.bfloat16)
    partial_grad = jnp.einsum(
        "rh,dh->rd", grad_pre, local_in, preferred_element_type=jnp.float32
    ).astype(jnp.bfloat16)
    return partial_grad.reshape(row_part.shape)


def gather_groups(returned, groups):
    feature_width = returned.shape[-1]
    summed = jnp.sum(
        returned.reshape(groups, GROUP, CAP, feature_width).astype(jnp.float32), axis=1
    )
    return summed.reshape(groups * CAP, feature_width)


def per_device(
    handoff,
    saved_inputs,
    cotangent,
    ids_forward,
    gates_forward,
    ids_backward,
    gates_backward,
    weight_in,
    weight_out,
):
    highest = lax.Precision.HIGHEST
    groups = lax.axis_size("expert") // GROUP
    segment_index = lax.axis_index("segment")
    last_segment = lax.axis_size("segment") - 1
    arrived = shifted(handoff, "segment", 1)
    inputs = jnp.where(segment_index == 0, handoff, arrived)[0]
    returned = shifted(cotangent, "segment", -1)
    upstream = jnp.where(segment_index == last_segment, cotangent, returned)[0]
    local_in = weight_in[0]
    local_out = weight_out[0]
    select_f, weigh_f = slot_tables(ids_forward[0], gates_forward[0], groups)
    picked = jnp.dot(
        select_f.astype(jnp.bfloat16), inputs, preferred_element_type=jnp.float32
    ).astype(jnp.bfloat16)
    select_b, weigh_b = slot_tables(ids_backward[0], gates_backward[0], groups)
    rows_back = jnp.dot(
        select_b.astype(jnp.bfloat16), saved_inputs[0], preferred_element_type=jnp.float32
    ).astype(jnp.bfloat16)
    grads_out = jnp.dot(
        weigh_b, upstream.astype(jnp.float32), precision=highest, preferred_element_type=jnp.float32
    ).astype(jnp.bfloat16)
    backward_stack = jnp.stack([rows_back, grads_out])
    arriving_f = lax.all_to_all(
        pack_direct(picked[None], groups), "expert", split_axis=1, concat_axis=1, tiled=True
    )
    arriving_b = lax.all_to_all(
        pack_direct(backward_stack, groups), "expert", split_axis=1, concat_axis=1, tiled=True
    )
    partial_f = expert_forward(arriving_f[0], local_in, local_out)
    back_f = lax.all_to_all(partial_f, "expert", split_axis=0, concat_axis=0, tiled=True)
    combined = gather_groups(back_f, groups)
    expert_mix = jnp.dot(
        weigh_f.T, combined, precision=highest, preferred_element_type=jnp.float32
    ).astype(jnp.bfloat16)
    partial_b = expert_backward(arriving_b[0], arriving_b[1], local_in, local_out)
    back_b = lax.all_to_all(partial_b, "expert", split_axis=0, concat_axis=0, tiled=True)
    slot_grads = gather_groups(back_b, groups)
    input_grads = jnp.dot(
        select_b.T, slot_grads, precision=highest, preferred_element_type=jnp.float32
    ).astype(jnp.bfloat16)
    return (expert_mix[None], input_grads[None])


MESH = pl.DeviceIdType.MESH
BLOCK = 16
THIRDS = 3
PARTS = 2
LANES = 128
GATHER_CROSS = (0,)
REDUCE_CROSS = (0, 1)
CORNER = (1, 2)


def flipped(position, mask):
    bit = 1
    while bit <= mask:
        if mask & bit:
            position = position + bit * (1 - 2 * ((position // bit) % 2))
        bit *= 2
    return position


def exchange_kernel(
    planes,
    chunk,
    ids_f_hbm,
    gates_f_hbm,
    ids_b_hbm,
    gates_b_hbm,
    handoff,
    saved,
    cotangent,
    weight_in,
    weight_out,
    sums,
    places,
    gate_wide,
    rows_x,
    rows_s,
    w_first,
    w_second,
    blocks,
    req_send,
    req_recv,
    late_send,
    slope,
    y_send,
    y_keep,
    y_recv,
    cross_keep,
    cross_recv,
    z_send,
    z_recv,
    own_sum,
    ids_f,
    gates_f,
    ids_b,
    gates_b,
    local_sem,
    send_sem,
    recv_sem,
):
    segment = lax.axis_index("segment")
    expert = lax.axis_index("expert")
    row_count, width = rows_x.shape
    hidden = weight_out.shape[0]
    tail = chunk // CAP
    rest = THIRDS * chunk

    def at_expert(mask):
        return {"expert": flipped(expert, mask)}

    def at_other(k):
        return {"segment": 1 - segment, "expert": flipped(expert, 4 * k)}

    sibling = at_expert(1)
    across = at_expert(2)
    mates = [None] + [at_expert(4 * k) for k in range(1, planes)]
    others = [at_other(k) for k in range(planes)]

    barrier = pltpu.get_barrier_semaphore()
    plane = expert // 4
    inner = (plane > 0) & (plane < planes - 1)
    partners = [across, sibling, others[0]] + mates[1 : planes - 1]
    for partner in partners:
        pl.semaphore_signal(barrier, inc=1, device_id=partner, device_id_type=MESH)

    @pl.when(inner)
    def _():
        pl.semaphore_signal(barrier, inc=1, device_id=mates[-1], device_id_type=MESH)


    tables = [
        pltpu.make_async_copy(source, target, local_sem.at[4 + i])
        for i, (source, target) in enumerate(
            [(ids_f_hbm, ids_f), (gates_f_hbm, gates_f), (ids_b_hbm, ids_b), (gates_b_hbm, gates_b)]
        )
    ]
    for table_copy in tables:
        table_copy.start()

    @pl.when(segment == 0)
    def _():
        pltpu.make_async_copy(handoff, rows_x, local_sem.at[0]).start()

    @pl.when(segment != 0)
    def _():
        pltpu.make_async_copy(cotangent, rows_x, local_sem.at[0]).start()

    load_x = pltpu.make_async_copy(handoff, rows_x, local_sem.at[0])
    load_s = pltpu.make_async_copy(saved, rows_s, local_sem.at[1])
    load_in = pltpu.make_async_copy(weight_in, w_first.at[0, :, 0:hidden], local_sem.at[2])
    load_out = pltpu.make_async_copy(weight_out, w_second.at[0, 0:hidden, :], local_sem.at[3])
    load_s.start()
    load_in.start()
    load_out.start()

    count = [0]

    def landing():
        count[0] += 1
        return recv_sem.at[count[0] - 1]

    def remote(source, target, device, leaving, arriving):
        return pltpu.make_async_remote_copy(
            src_ref=source,
            dst_ref=target,
            send_sem=leaving,
            recv_sem=arriving,
            device_id=device,
            device_id_type=MESH,
        )

    def start_inner(copies):
        @pl.when(inner)
        def _():
            for copy in copies:
                copy.start()

    parts = range(PARTS)
    edges = [CAP * i // PARTS for i in range(PARTS + 1)]
    cuts = [slice(tail * low, tail * high) for low, high in zip(edges[:-1], edges[1:])]

    request = remote(req_send, req_recv, others[0], send_sem.at[0], landing())
    give_in = remote(weight_in, w_first.at[0, :, hidden : 2 * hidden], sibling, send_sem.at[1], landing())
    give_out = remote(weight_out, w_second.at[0, hidden : 2 * hidden, :], sibling, send_sem.at[2], landing())

    def ship(source, target, device, leaving, arriving):
        return [
            remote(source.at[:, cut], target.at[:, cut], device, leaving, arriving[part])
            for part, cut in enumerate(cuts)
        ]

    def block(kind, k, side=0):
        return blocks.at[(kind * planes + k) * 2 + side]

    far = planes - 1
    gathers, inners, reduces, fars, corners = [send_sem.at[i] for i in range(3, 8)]
    land_z = [[[landing() for part in parts] for k in range(planes)] for kind in range(3)]
    land_y = [[landing()] * PARTS for kind in range(3)]
    land_near = [[landing() for part in parts] for kind in range(3)]
    land_cross = [[landing() for part in parts] for o in range(2)]
    land_back_y = [[[landing() for part in parts] for k in range(planes)] for o in range(2)]
    land_back_z = [[landing()] * PARTS for o in range(2)]
    gather_z = []
    for kind in range(3):
        sources = [late_send if kind == 2 else block(kind, 0)] * planes
        targets = others if kind == 2 else mates
        gather_z.append(
            [
                None
                if targets[k] is None
                else ship(sources[k], block(kind, k), targets[k], inners if k == far else gathers, land_z[kind][k])
                for k in range(planes)
            ]
        )
    forward_z = [ship(block(kind, 2), block(kind, far), mates[1], inners, land_z[kind][far]) for kind in range(3)]
    gather_y = [
        [
            ship(block(kind, k), block(kind, k, 1), across, fars if k == far else gathers, land_y[kind] if k else land_near[kind])
            for k in range(planes)
        ]
        for kind in range(3)
    ]
    corner_z = [
        ship(block(kind, 2), block(kind, far, 1), at_expert(6), corners, land_y[kind]) for kind in range(3)
    ]
    gather_cross = [
        ship(block(kind, 0, 1), block(kind, 1, 1), mates[1], gathers, land_y[kind]) for kind in range(3)
    ]
    reduce_cross = [ship(y_send.at[o, 1], cross_recv.at[o], mates[1], reduces, land_cross[o]) for o in range(2)]
    reduce_y = [
        [ship(y_send.at[o, k], y_recv.at[o, k], across, reduces, land_back_y[o][k]) for k in range(planes)]
        for o in range(2)
    ]
    reduce_z = [
        [None] + [ship(z_send.at[o, k], z_recv.at[o, k], mates[k], reduces, land_back_z[o]) for k in range(1, planes)]
        for o in range(2)
    ]

    def whole(number, leaving, arriving):
        return remote(blocks.at[0:number], blocks.at[0:number], across, leaving, arriving)

    for table_copy in tables:
        table_copy.wait()
    earlier = jnp.where(
        lax.broadcasted_iota(jnp.int32, (row_count, row_count), 0)
        < lax.broadcasted_iota(jnp.int32, (row_count, row_count), 1),
        1.0,
        0.0,
    ).astype(jnp.bfloat16)
    block_row = lax.broadcasted_iota(jnp.int32, (BLOCK, row_count), 0)
    third = sum((block_row >= CAP * q).astype(jnp.int32) for q in range(1, THIRDS + 1))
    slot = block_row - CAP * third

    def ranks(ids, gates):
        first, second = ids[0:1, :] == 0, ids[1:2, :] == 0
        member = jnp.where(first | second, 1.0, 0.0)
        gate = jnp.where(first, gates[0:1, :], 0.0) + jnp.where(second, gates[1:2, :], 0.0)
        wide = jnp.broadcast_to(member, (BLOCK, row_count))
        rank = jnp.dot(wide.astype(jnp.bfloat16), earlier, preferred_element_type=jnp.float32)
        placed = jnp.where((slot == rank.astype(jnp.int32)) & (third < THIRDS), wide, 0.0)
        return placed, gate

    placed_f, gate_f = ranks(ids_f, gates_f)
    placed_b, gate_b = ranks(ids_b, gates_b)
    later = (segment * jnp.ones((), jnp.int32)).astype(jnp.float32)
    scaled_b = placed_b * gate_b
    asked = scaled_b * (1.0 - later) + placed_f * later
    mine = placed_f * (1.0 - later) + scaled_b * later
    req_send[...] = jnp.concatenate([asked, jnp.zeros((BLOCK, LANES - row_count), jnp.float32)], axis=1)

    @pl.when(inner)
    def _():
        pl.semaphore_wait(barrier, len(partners) + 1)

    @pl.when(jnp.logical_not(inner))
    def _():
        pl.semaphore_wait(barrier, len(partners))

    request.start()

    def pick(weights, rows_ref, target):
        ending = jnp.concatenate(
            [jnp.where(block_row == BLOCK - 1, weights[i : i + 1, :], 0.0) for i in range(CAP)], axis=0
        )

        def product(chosen, columns):
            return jnp.dot(
                jnp.where(chosen, 1.0, 0.0).astype(jnp.bfloat16),
                rows_ref[:, columns],
                preferred_element_type=jnp.float32,
            )

        scale = jnp.sum(weights, axis=1, keepdims=True)
        chosen = [(weights != 0.0) & (third == q) for q in range(THIRDS)]
        last = product(ending != 0.0, slice(rest, width)) * jnp.sum(ending, axis=1, keepdims=True)
        for i in range(CAP):
            total = sum(
                product(chosen[q], slice(q * chunk + i * tail, q * chunk + (i + 1) * tail)) for q in range(THIRDS)
            )
            value = total * scale + last[i * BLOCK : (i + 1) * BLOCK]
            target[:, i * tail : (i + 1) * tail] = value.astype(jnp.bfloat16)

    def spread(kind):
        for part in parts:
            gather_y[kind][0][part].start()
            for k in range(1, far):
                gather_z[kind][k][part].start()
        start_inner(gather_z[kind][far])

    load_x.wait()
    pick(mine, rows_x, block(0, 0))
    spread(0)
    load_s.wait()
    pick(placed_b, rows_s, block(1, 0))
    spread(1)
    give_in.start()
    give_out.start()
    turn = 512 if width % 512 == 0 else LANES

    def transpose(low, share=0, shares=1):
        half = slice(low, low + hidden)

        def step(number, carry):
            piece = pl.ds(pl.multiple_of(number * turn, turn), turn)
            w_first[1, piece, half] = w_second[0, half, piece].T
            w_second[1, half, piece] = w_first[0, piece, half].T
            return carry

        steps = width // turn
        lax.fori_loop(steps * share // shares, steps * (share + 1) // shares, step, 0)

    load_in.wait()
    load_out.wait()
    transpose(0)
    request.wait_recv()
    pick(req_recv[:, 0:row_count], rows_x, late_send)
    for part in parts:
        for k in range(far):
            gather_z[2][k][part].start()
    start_inner(gather_z[2][far])

    def relay(kind, k, corner=False):
        for part in parts:
            gather_z[kind][k][part].wait_recv()
            if k == 2:
                start_inner([forward_z[kind][part]] + ([corner_z[kind][part]] if kind in CORNER else []))
            if not corner and (k != 1 or part not in GATHER_CROSS):
                gather_y[kind][k][part].start()

    def cross(kind):
        for part in parts:
            gather_y[kind][0][part].wait_recv()
            if part in GATHER_CROSS:
                gather_cross[kind][part].start()

    def relays(outer_order, inner_order):
        @pl.when(inner)
        def _():
            for kind, k in inner_order:
                relay(kind, k)

        @pl.when(jnp.logical_not(inner))
        def _():
            for kind, k in outer_order:
                relay(kind, k, k == far and kind in CORNER)

    relays([(0, 1), (0, 2), (1, 1)], [(0, 1), (0, 2), (0, 3), (1, 1)])
    cross(0)
    cross(1)
    relays([(2, 0)], [(1, 2), (2, 0), (1, 3)])
    give_in.wait_recv()
    give_out.wait_recv()
    transpose(hidden, 0, 2)
    relays([(1, 2), (2, 1)], [(2, 1)])
    transpose(hidden, 1, 2)
    relays([(0, 3), (2, 2)], [(2, 2), (2, 3)])
    cross(2)
    unit = jnp.where(
        lax.broadcasted_iota(jnp.int32, (row_count, row_count), 0)
        == lax.broadcasted_iota(jnp.int32, (row_count, row_count), 1),
        1.0,
        0.0,
    )
    by_row = (((1,), (1,)), ((), ()))
    for i, placed in enumerate([placed_f, placed_b]):
        places[i] = lax.dot_general(
            unit.astype(jnp.bfloat16),
            placed.astype(jnp.bfloat16),
            by_row,
            preferred_element_type=jnp.float32,
        ).astype(jnp.bfloat16)
    gate_wide[...] = lax.dot_general(
        unit,
        jnp.broadcast_to(gate_f, (LANES, row_count)),
        by_row,
        precision=lax.Precision.HIGHEST,
        preferred_element_type=jnp.float32,
    )

    batch = 2 * planes * BLOCK
    place = lax.broadcasted_iota(jnp.int32, (batch, 2 * hidden), 0) % BLOCK

    def arrived(kind):
        whole(planes - 1, gathers, land_y[kind][0]).wait_recv()

    def contract(kind, side):
        gathered = blocks[2 * planes * kind : 2 * planes * (kind + 1)].reshape(batch, chunk)

        def product(columns, rows):
            return jnp.dot(gathered[:, columns], w_first[side, rows, :], preferred_element_type=jnp.float32)

        value = product(slice(0, chunk), slice(0, chunk))
        for q in range(1, THIRDS):
            value = value + pltpu.roll(
                product(slice(0, chunk), slice(q * chunk, (q + 1) * chunk)), batch - CAP * q, 0
            )
        for i in range(CAP):
            last = product(slice(i * tail, (i + 1) * tail), slice(rest, width))
            value = value + jnp.where(place == i, pltpu.roll(last, batch - (BLOCK - 1 - i), 0), 0.0)
        return value

    def sigmoid(value):
        return 1.0 / (1.0 + jnp.exp(-value))

    order = [k for k in range(planes - 1, -1, -1)]

    def expand(value, side, o):
        value = jnp.where(place < CAP, value, 0.0)
        left = [value.astype(jnp.bfloat16)]
        left += [pltpu.roll(value, CAP * q, 0).astype(jnp.bfloat16) for q in range(1, THIRDS)]
        for part in parts:
            for i in range(edges[part], edges[part + 1]):
                piece = slice(i * tail, (i + 1) * tail)
                total = sum(
                    jnp.dot(
                        left[q],
                        w_second[side, :, q * chunk + i * tail : q * chunk + (i + 1) * tail],
                        preferred_element_type=jnp.float32,
                    )
                    for q in range(THIRDS)
                )
                last = jnp.where(place == BLOCK - 1, pltpu.roll(value, BLOCK - 1 - i, 0), 0.0)
                total = total + jnp.dot(
                    last.astype(jnp.bfloat16), w_second[side, :, rest:width], preferred_element_type=jnp.float32
                )
                total = total.reshape(planes, 2, BLOCK, tail)
                y_keep[o, :, :, piece] = total[:, 0]
                y_send[o, 1:planes, :, piece] = total[1:planes, 1].astype(jnp.bfloat16)
                if part in REDUCE_CROSS:
                    cross_keep[o, :, piece] = total[0, 1]
                    z_send[o, 1, :, piece] = total[1, 0].astype(jnp.bfloat16)
                else:
                    y_send[o, 0, :, piece] = total[0, 1].astype(jnp.bfloat16)
            if part in REDUCE_CROSS:
                reduce_cross[o][part].start()
            for k in order:
                if k > 1 or part not in REDUCE_CROSS:
                    reduce_y[o][k][part].start()
            if part in REDUCE_CROSS:
                reduce_z[o][1][part].start()

    def join(o, part):
        cut = cuts[part]
        for k in order:
            if k > 1 or (k == 1 and part not in REDUCE_CROSS):
                reduce_y[o][k][part].wait_recv()
                total = y_keep[o, k, :, cut] + y_recv[o, k, :, cut].astype(jnp.float32)
                z_send[o, k, :, cut] = total.astype(jnp.bfloat16)
                reduce_z[o][k][part].start()

    def join_cross(o, part):
        if part in REDUCE_CROSS:
            cut = cuts[part]
            reduce_cross[o][part].wait_recv()
            total = cross_keep[o, :, cut] + cross_recv[o, :, cut].astype(jnp.float32)
            y_send[o, 0, :, cut] = total.astype(jnp.bfloat16)
            reduce_y[o][0][part].start()

    def join_own(o, part):
        cut = cuts[part]
        reduce_y[o][0][part].wait_recv()
        own_sum[o, :, cut] = y_keep[o, 0, :, cut] + y_recv[o, 0, :, cut].astype(jnp.float32)

    arrived(0)
    first = contract(0, segment)
    relays([(1, 3)], [])
    arrived(1)
    pre = contract(1, 0)
    gate = sigmoid(pre)
    slope[...] = gate * (1.0 + pre * (1.0 - gate))
    expand(first * sigmoid(first) * (1.0 - later) + first * slope[...] * later, segment, 0)
    relays([(2, 3)], [])
    arrived(2)
    last = contract(2, 1 - segment)
    expand(last * slope[...] * (1.0 - later) + last * sigmoid(last) * later, 1 - segment, 1)
    for part in parts:
        join(0, part)

    @pl.when(jnp.logical_not(inner))
    def _():
        for part in parts:
            join_cross(0, part)

    for part in parts:
        join(1, part)

    @pl.when(inner)
    def _():
        for part in parts:
            join_cross(0, part)

    for part in parts:
        join_cross(1, part)
    for o in range(2):
        for part in parts:
            join_own(o, part)
    for o in range(2):
        whole(planes - 1, reduces, land_back_z[o][0]).wait_recv()
        total = own_sum[o]
        for k in range(1, planes):
            total = total + z_recv[o, k].astype(jnp.float32)
        sums[segment if o == 0 else 1 - segment] = total.astype(jnp.bfloat16)
    request.wait_send()
    give_in.wait_send()
    give_out.wait_send()
    whole(5 * planes - 4, gathers, land_y[0][0]).wait_send()
    whole(4 * planes - 2, reduces, land_y[0][0]).wait_send()

    @pl.when(inner)
    def _():
        whole(6, inners, land_y[0][0]).wait_send()
        whole(3, fars, land_y[0][0]).wait_send()
        if CORNER:
            whole(len(CORNER), corners, land_y[0][0]).wait_send()

    @pl.when(jnp.logical_not(inner))
    def _():
        if len(CORNER) < 3:
            whole(3 - len(CORNER), fars, land_y[0][0]).wait_send()


def scatter_kernel(chunk, sums, places, gate_wide, mixed, grads, out_f, out_b, sems):
    width = out_f.shape[1]
    column = lax.broadcasted_iota(jnp.int32, places.shape[1:], 1)
    gate = gate_wide[:, 0:1]
    tail = chunk // CAP
    copies = []

    def product(i, chosen, columns):
        return jnp.dot(chosen.astype(jnp.bfloat16), sums[i, :, columns], preferred_element_type=jnp.float32)

    for i, (held, out) in enumerate([(out_f, mixed), (out_b, grads)]):
        placed = places[i].astype(jnp.float32)

        def put(columns, value):
            held[:, columns] = (value * gate if i == 0 else value).astype(jnp.bfloat16)

        def send(columns):
            copies.append(
                pltpu.make_async_copy(held.at[:, columns], out.at[:, columns], sems.at[len(copies)])
            )
            copies[-1].start()

        for q in range(THIRDS):
            inside = (column >= CAP * q) & (column < CAP * (q + 1))
            put(slice(q * chunk, (q + 1) * chunk), product(i, jnp.where(inside, placed, 0.0), slice(0, chunk)))
            if q < THIRDS - 1:
                send(slice(q * chunk, (q + 1) * chunk))
        put(
            slice(THIRDS * chunk, width),
            sum(
                product(
                    i,
                    jnp.where(column == BLOCK - 1, placed[:, slot : slot + 1], 0.0),
                    slice(slot * tail, (slot + 1) * tail),
                )
                for slot in range(CAP)
            ),
        )
        send(slice((THIRDS - 1) * chunk, width))
    for copy in copies:
        copy.wait()


def exchange(planes, handoff, saved_inputs, cotangent, ids_forward, gates_forward, ids_backward, gates_backward, weight_in, weight_out):
    rows, width = handoff.shape[1:]
    hidden = weight_out.shape[1]
    chunk = width // BLOCK * CAP
    bf16, f32 = jnp.bfloat16, jnp.float32
    landings = 3 + PARTS * 5 * planes + 5 + PARTS * 5
    vmem = pl.BlockSpec(memory_space=pltpu.VMEM)
    hbm = pl.BlockSpec(memory_space=pl.ANY)
    sums, places, gate_wide = pl.pallas_call(
        functools.partial(exchange_kernel, planes, chunk),
        out_shape=[
            pltpu.VMEM((2, BLOCK, chunk), bf16),
            pltpu.VMEM((2, rows, BLOCK), bf16),
            pltpu.VMEM((rows, LANES), f32),
        ],
        in_specs=[hbm] * 9,
        out_specs=[vmem] * 3,
        scratch_shapes=[
            pltpu.VMEM((rows, width), bf16),
            pltpu.VMEM((rows, width), bf16),
            pltpu.VMEM((2, width, 2 * hidden), bf16),
            pltpu.VMEM((2, 2 * hidden, width), bf16),
            pltpu.VMEM((6 * planes, BLOCK, chunk), bf16),
            pltpu.VMEM((BLOCK, LANES), f32),
            pltpu.VMEM((BLOCK, LANES), f32),
            pltpu.VMEM((BLOCK, chunk), bf16),
            pltpu.VMEM((2 * planes * BLOCK, 2 * hidden), f32),
            pltpu.VMEM((2, planes, BLOCK, chunk), bf16),
            pltpu.VMEM((2, planes, BLOCK, chunk), f32),
            pltpu.VMEM((2, planes, BLOCK, chunk), bf16),
            pltpu.VMEM((2, BLOCK, chunk), f32),
            pltpu.VMEM((2, BLOCK, chunk), bf16),
            pltpu.VMEM((2, planes, BLOCK, chunk), bf16),
            pltpu.VMEM((2, planes, BLOCK, chunk), bf16),
            pltpu.VMEM((2, BLOCK, chunk), f32),
            pltpu.VMEM((2, rows), jnp.int32),
            pltpu.VMEM((2, rows), f32),
            pltpu.VMEM((2, rows), jnp.int32),
            pltpu.VMEM((2, rows), f32),
            pltpu.SemaphoreType.DMA((8,)),
            pltpu.SemaphoreType.DMA((8,)),
            pltpu.SemaphoreType.DMA((landings,)),
        ],
        compiler_params=pltpu.CompilerParams(
            collective_id=0, has_side_effects=True
        ),
    )(
        ids_forward[0].T,
        gates_forward[0].T,
        ids_backward[0].T,
        gates_backward[0].T,
        handoff[0],
        saved_inputs[0],
        cotangent[0],
        weight_in[0],
        weight_out[0],
    )
    mixed, grads = pl.pallas_call(
        functools.partial(scatter_kernel, chunk),
        out_shape=[jax.ShapeDtypeStruct((rows, width), bf16)] * 2,
        in_specs=[vmem] * 3,
        out_specs=[hbm] * 2,
        scratch_shapes=[
            pltpu.VMEM((rows, width), bf16),
            pltpu.VMEM((rows, width), bf16),
            pltpu.SemaphoreType.DMA((2 * THIRDS,)),
        ],
    )(*[pltpu.with_memory_space_constraint(x, pltpu.VMEM) for x in (sums, places, gate_wide)])
    return (mixed[None], grads[None])


def device_body(mesh):
    segments, experts = mesh.shape["segment"], mesh.shape["expert"]
    planes = experts // 4
    if segments == 2 and experts == GROUP and planes == 4:
        return functools.partial(exchange, planes)
    return per_device


def solution(mesh):
    return jax.shard_map(
        device_body(mesh),
        mesh=mesh,
        in_specs=(
            P("segment", "expert", None),
            P("segment", "expert", None),
            P("segment", "expert", None),
            P("segment", "expert", None),
            P("segment", "expert", None),
            P("segment", "expert", None),
            P("segment", "expert", None),
            P("segment", None, "expert"),
            P("segment", "expert", None),
        ),
        out_specs=(P("segment", "expert", None), P("segment", "expert", None)),
        check_vma=False,
    )
```
